32 devices in a mesh: gx: 4 (over z), gz: 4 (over y, core), sa: 2 (over x).
Axes of the slice: x: 2, y: 2, z: 4, core: 2. Of those that a mesh axis runs over, the one named last changes fastest.
Arguments:
- forcing: float32 [3, 8, 128, 32, 256], P(None, 'sa', 'gx', 'gz'), may hold values from -60 to 60
- velocity: float32 [256], replicated, may hold values from 0.3 to 1.2
- wall_solve: float32 [256, 256], replicated, may hold values from -1 to 1.7
Outputs:
- basis: float32 [3, 8, 128, 32, 256], P(None, 'sa', 'gx', 'gz')
- factor: float32 [8, 8], replicated
The draws below stay inside these ranges and needn't reach their ends.
All inputs are finite; a program needn't handle non-finite values.
Results may differ from the reference program's by a relative error of at most 0.00015.
Values sent between devices are 32-bit elements; how exact they have to be, the bound alone decides.
No kernel may reach another device: no remote copies, remote signals or barrier semaphores. Data moves between devices by JAX's collectives and lax.ppermute only.
A program may use at most 64 MiB of HBM per device.

```python
import math
import jax
import jax.numpy as jnp
from jax import lax

NY = 256
NX = 128
NZ = 32
SKETCH = 8


def draw_forcing(key, part):
    noise_key = jax.random.fold_in(key, 11)
    mixing_key = jax.random.fold_in(key, 13)
    shared_key = jax.random.fold_in(key, 14)
    place_x = jnp.arange(NX, dtype=jnp.float32) / NX
    place_z = jnp.arange(NZ, dtype=jnp.float32) / NZ
    shape = (3, SKETCH + 1, NX, NZ, NY)
    noise = jnp.clip(jax.random.normal(noise_key, shape, jnp.float32), -6.0, 6.0)
    envelope = jnp.exp(0.55 * (place_x[:, None] + place_z[None, :]))
    fields = noise * envelope[:, :, None]
    spread = 0.8 / (SKETCH - 1)
    unit_matrix = jnp.eye(SKETCH, dtype=jnp.float32)
    off_terms = jax.random.uniform(mixing_key, (SKETCH, SKETCH), jnp.float32, -spread, spread) * (1.0 - unit_matrix)
    mixing = unit_matrix + off_terms
    shared_weight = jax.random.uniform(shared_key, (SKETCH,), jnp.float32, 0.5, 0.9)
    value = shared_weight[None, :, None, None, None] * fields[:, SKETCH:SKETCH + 1]
    for source in range(SKETCH):
        value = value + mixing[:, source][None, :, None, None, None] * fields[:, source:source + 1]
    return value / 2.7


def draw_wall_solve(key, part):
    first_key, second_key = jax.random.split(key)
    diagonal = 1.0 + 0.3 * jax.random.uniform(first_key, (NY,), jnp.float32)
    spread = jnp.clip(jax.random.normal(second_key, (NY, NY), jnp.float32), -4.0, 4.0)
    return jnp.diag(diagonal) + spread * (0.5 / math.sqrt(NY))


def setup_inputs(seed: int = 0) -> dict:
    keys = jax.random.split(jax.random.key(seed), 4)
    return {
        "forcing": draw_forcing(jax.random.fold_in(keys[3], 71), 0),
        "velocity": jnp.clip(jnp.exp(jax.random.uniform(keys[1], (NY,), jnp.float32, math.log(0.3), math.log(1.2))), 0.3, 1.2),
        "wall_solve": draw_wall_solve(jax.random.fold_in(keys[3], 71), 0),
    }


step_length = 0.4
viscosity = 0.2

def shear_of(velocity):
    inner = (velocity[2:] - velocity[:-2]) * 0.5
    return jnp.concatenate([velocity[1:2] - velocity[0:1], inner, velocity[-1:] - velocity[-2:-1]])

def upper_factor(gram):
    order_size = gram.shape[0]
    column_ids = jnp.arange(order_size)
    row_list = []
    for pivot_index in range(order_size):
        current_row = gram[pivot_index]
        for other_index in range(pivot_index):
            current_row = current_row - row_list[other_index][pivot_index] * row_list[other_index]
        current_row = jnp.where(column_ids >= pivot_index, current_row, jnp.zeros_like(current_row)) / jnp.sqrt(current_row[pivot_index])
        row_list.append(current_row)
    return jnp.stack(row_list)

def upper_inverse(factor):
    order_size = factor.shape[0]
    identity_rows = jnp.eye(order_size, dtype=factor.dtype)
    row_list = [None] * order_size
    for pivot_index in range(order_size - 1, -1, -1):
        current_row = identity_rows[pivot_index]
        for other_index in range(pivot_index + 1, order_size):
            current_row = current_row - factor[pivot_index, other_index] * row_list[other_index]
        row_list[pivot_index] = current_row / factor[pivot_index, pivot_index]
    return jnp.stack(row_list)

def operate(field, velocity, shear_rate, adjoint):
    east_side = jnp.roll(field, -1, axis=2)
    west_side = jnp.roll(field, 1, axis=2)
    north_side = jnp.roll(field, -1, axis=3)
    south_side = jnp.roll(field, 1, axis=3)
    direction = 1.0 if adjoint else -1.0
    change = direction * velocity * (east_side - west_side) * 0.5 + viscosity * (east_side + west_side + north_side + south_side - 4.0 * field)
    if adjoint:
        return change.at[1].add(-shear_rate * field[0])
    return change.at[0].add(-shear_rate * field[1])

def reference(forcing, velocity, wall_solve):
    shear_rate = shear_of(velocity)
    current = forcing
    for repeat in range(2):
        current = jnp.matmul(current + step_length * (operate(current, velocity, shear_rate, False) + forcing), wall_solve, precision=lax.Precision.HIGHEST)
    entries = 3 * NX * NZ * NY
    partial_value = lax.optimization_barrier(jnp.sum(current * current, axis=(0, 2, 3, 4)))
    scales = jnp.sqrt(partial_value / entries + 1e-06)
    response = current / scales[None, :, None, None, None]
    current = response
    for repeat in range(2):
        solved = jnp.matmul(current, wall_solve.T, precision=lax.Precision.HIGHEST)
        current = solved + step_length * operate(solved, velocity, shear_rate, True) + step_length * response
    gram = jnp.einsum('cixzy,cjxzy->ij', current, current, precision=lax.Precision.HIGHEST) / entries
    factor = upper_factor(gram)
    inverse = upper_inverse(factor)
    basis = jnp.einsum('cixzy,ij->cjxzy', current, inverse, precision=lax.Precision.HIGHEST)
    return (basis, factor)
```

```python
import functools

import jax
import jax.numpy as jnp
from jax import lax
from jax.experimental import pallas as pl
from jax.experimental.pallas import tpu as pltpu
from jax.sharding import PartitionSpec as P

step_length = 0.4
viscosity = 0.2
VMEM_LIMIT = 56 * 1024 * 1024
X_CHUNK = 8


def shear_of(velocity):
    inner = (velocity[2:] - velocity[:-2]) * 0.5
    return jnp.concatenate([velocity[1:2] - velocity[0:1], inner, velocity[-1:] - velocity[-2:-1]])


def split_halves(value):
    high = value.astype(jnp.bfloat16)
    low = (value - high.astype(jnp.float32)).astype(jnp.bfloat16)
    return high, low


def wall_product(high, low, wall_ref):
    dot = functools.partial(jnp.dot, preferred_element_type=jnp.float32)
    return dot(low, wall_ref[0]) + dot(high, wall_ref[1]) + dot(high, wall_ref[0])


def stencil_chunk(cur, comp, x0, xlo, xhi, zlo, zhi, coef, adjoint):
    nx = cur.shape[2]
    x1 = x0 + X_CHUNK
    mid = cur[comp, 0, x0:x1]
    if x0 == 0:
        west = jnp.concatenate([xlo[comp, 0][None], cur[comp, 0, 0 : x1 - 1]], axis=0)
    else:
        west = cur[comp, 0, x0 - 1 : x1 - 1]
    if x1 == nx:
        east = jnp.concatenate([cur[comp, 0, x0 + 1 : x1], xhi[comp, 0][None]], axis=0)
    else:
        east = cur[comp, 0, x0 + 1 : x1 + 1]
    nz = mid.shape[1]
    rows = lax.broadcasted_iota(jnp.int32, mid.shape, 1)
    low_face = jnp.broadcast_to(zlo[comp, 0, x0:x1][:, None, :], mid.shape)
    high_face = jnp.broadcast_to(zhi[comp, 0, x0:x1][:, None, :], mid.shape)
    south = jnp.where(rows == 0, low_face, pltpu.roll(mid, 1, 1))
    north = jnp.where(rows == nz - 1, high_face, pltpu.roll(mid, nz - 1, 1))
    side = viscosity * step_length
    plus, minus = coef[0][None], coef[1][None]
    if adjoint:
        plus, minus = minus, plus
    value = (1.0 - 4.0 * side) * mid + plus * east + minus * west + side * (north + south)
    if adjoint and comp == 1:
        value = value - coef[2][None] * cur[0, 0, x0:x1]
    if not adjoint and comp == 0:
        value = value - coef[2][None] * cur[1, 0, x0:x1]
    return value


def put_faces(result, comp, first_x, last_x, first_z, last_z):
    nx, nz = result.shape[0], result.shape[1]
    first_x[comp, 0] = result[0]
    last_x[comp, 0] = result[nx - 1]
    first_z[comp, 0] = result[:, 0, :]
    last_z[comp, 0] = result[:, nz - 1, :]


def stage_body(kind, *refs):
    if kind == "adjoint_last":
        half_ref, *refs = refs
    cur, src, xlo, xhi, zlo, zhi, coef, wall, *rest = refs
    nx, nz, ny = cur.shape[2:]
    if kind == "forward_first":
        out, fx, lx, fz, lz, high, low = rest
    elif kind == "forward_last":
        out, solved, squares, fx, lx, fz, lz, high, low = rest
    elif kind == "adjoint_first":
        out, fx, lx, fz, lz, high, low = rest
    else:
        keep, send = rest
    adjoint = kind.startswith("adjoint")
    for comp in range(3):
        for x0 in range(0, nx, X_CHUNK):
            value = stencil_chunk(cur, comp, x0, xlo, xhi, zlo, zhi, coef, adjoint)
            value = value + step_length * src[comp, 0, x0 : x0 + X_CHUNK]
            if kind == "adjoint_last":
                half_x = nx // 2
                own = half_ref[0] == (1 if x0 >= half_x else 0)
                spot = x0 % half_x

                @pl.when(own)
                def _():
                    keep[comp, 0, spot : spot + X_CHUNK] = value

                @pl.when(jnp.logical_not(own))
                def _():
                    send[comp, 0, spot : spot + X_CHUNK] = value
            else:
                h, l = split_halves(value.reshape(X_CHUNK * nz, ny))
                spot = (comp * nx + x0) * nz
                high[spot : spot + X_CHUNK * nz] = h
                low[spot : spot + X_CHUNK * nz] = l
    if kind == "adjoint_last":
        return
    size = nx * nz
    total = None
    for comp in range(3):
        part = slice(comp * size, (comp + 1) * size)
        result = wall_product(high[part], low[part], wall.at[pl.ds(2, 2)] if adjoint else wall)
        tile = result.reshape(nx, nz, ny)
        out[comp, 0] = tile
        if kind == "forward_last":
            sums = jnp.sum(tile * tile, axis=0)
            total = sums if total is None else total + sums
            h, l = split_halves(result)
            result = wall_product(h, l, wall.at[pl.ds(2, 2)])
            tile = result.reshape(nx, nz, ny)
            solved[comp, 0] = tile
        put_faces(tile, comp, fx, lx, fz, lz)
    if kind == "forward_last":
        squares[0] = total


def run_stage(kind, cur, src, faces, coef, wall, half=None):
    three, columns, nx, nz, ny = cur.shape
    xlo, xhi, zlo, zhi = faces
    whole = pl.BlockSpec((three, 1, nx, nz, ny), lambda j, *_: (0, j, 0, 0, 0))
    half_spec = pl.BlockSpec((three, 1, nx // 2, nz, ny), lambda j, *_: (0, j, 0, 0, 0))
    x_face = pl.BlockSpec((three, 1, nz, ny), lambda j, *_: (0, j, 0, 0))
    z_face = pl.BlockSpec((three, 1, nx, ny), lambda j, *_: (0, j, 0, 0))
    fixed3 = pl.BlockSpec((3, nz, ny), lambda j, *_: (0, 0, 0))
    fixed4 = pl.BlockSpec((4, ny, ny), lambda j, *_: (0, 0, 0))
    square_spec = pl.BlockSpec((1, nz, ny), lambda j, *_: (j, 0, 0))
    f32 = jnp.float32
    field = jax.ShapeDtypeStruct(cur.shape, f32)
    half_field = jax.ShapeDtypeStruct((three, columns, nx // 2, nz, ny), f32)
    x_out = jax.ShapeDtypeStruct((three, columns, nz, ny), f32)
    z_out = jax.ShapeDtypeStruct((three, columns, nx, ny), f32)
    face_outs, face_specs = [x_out, x_out, z_out, z_out], [x_face, x_face, z_face, z_face]
    scratch = [pltpu.VMEM((three * nx * nz, ny), jnp.bfloat16)] * 2
    if kind == "forward_last":
        outs = [field, field, jax.ShapeDtypeStruct((columns, nz, ny), f32)] + face_outs
        specs = [whole, whole, square_spec] + face_specs
    elif kind == "adjoint_last":
        outs, specs, scratch = [half_field, half_field], [half_spec, half_spec], []
    else:
        outs, specs = [field] + face_outs, [whole] + face_specs
    in_specs = [whole, whole, x_face, x_face, z_face, z_face, fixed3, fixed4]
    operands = [cur, src, xlo, xhi, zlo, zhi, coef, wall]
    prefetch = 0
    if kind == "adjoint_last":
        prefetch, operands = 1, [half] + operands
    return pl.pallas_call(
        functools.partial(stage_body, kind),
        out_shape=outs,
        grid_spec=pltpu.PrefetchScalarGridSpec(
            num_scalar_prefetch=prefetch,
            grid=(columns,),
            in_specs=in_specs,
            out_specs=specs,
            scratch_shapes=scratch,
        ),
        compiler_params=pltpu.CompilerParams(vmem_limit_bytes=VMEM_LIMIT),
        name=kind,
    )(*operands)


def gram_body(half_ref, own, other, squares, out, acc, sums):
    step = pl.program_id(0)
    columns = own.shape[1]
    count = 2 * columns
    pairs = [(i, j) for i in range(count) for j in range(i, count)]

    @pl.when(step == 0)
    def _():
        acc[...] = jnp.zeros_like(acc)

    three, _, nx, nz, ny = own.shape
    for lane in range(0, ny, 128):

        def body(k, carry):
            comp = k // nx
            x = k - comp * nx
            cols = [own[comp, i, x, :, lane : lane + 128] for i in range(columns)]
            cols += [other[comp, i, x, :, lane : lane + 128] for i in range(columns)]
            return tuple(c + cols[i] * cols[j] for c, (i, j) in zip(carry, pairs))

        start = tuple(acc[p] for p in range(len(pairs)))
        done = lax.fori_loop(0, three * nx, body, start)
        for p in range(len(pairs)):
            acc[p] = done[p]

    @pl.when(step == pl.num_programs(0) - 1)
    def _():
        for p in range(len(pairs)):
            sums[p : p + 1] = jnp.sum(acc[p], axis=0, keepdims=True)
        spot = {}
        for p, (i, j) in enumerate(pairs):
            spot[i, j] = spot[j, i] = p
        lanes = lax.broadcasted_iota(jnp.int32, (count, 128), 1)
        rows = lax.broadcasted_iota(jnp.int32, (count, 128), 0)
        plain = jnp.zeros((count, 128), jnp.float32)
        moved = jnp.zeros((count, 128), jnp.float32)
        for i in range(count):
            stack = jnp.concatenate([sums[spot[i, j] : spot[i, j] + 1] for j in range(count)], axis=0)
            column = jnp.sum(stack, axis=1, keepdims=True)
            plain = jnp.where(lanes == i, column, plain)
            moved = jnp.where(lanes == (i + columns) % count, column, moved)
        norm_rows = [
            jnp.sum(squares[i, :, 0:128] + squares[i, :, 128:256], axis=0, keepdims=True) for i in range(columns)
        ]
        norm = jnp.sum(jnp.concatenate(norm_rows * 2, axis=0), axis=1, keepdims=True)
        plain = jnp.where(lanes == count, jnp.where(rows < columns, norm, 0.0), plain)
        moved = jnp.where(lanes == count, jnp.where(rows < columns, norm, 0.0), moved)
        moved = pltpu.roll(moved, columns, 0)
        out[...] = jnp.where(half_ref[0] == 0, plain, moved)


def run_gram(half, own, other, squares):
    three, columns, nx, nz, ny = own.shape
    steps = 4
    count = 2 * columns
    npairs = count * (count + 1) // 2
    block = pl.BlockSpec((three, columns, nx // steps, nz, ny), lambda k, *_: (0, 0, k, 0, 0))
    return pl.pallas_call(
        gram_body,
        out_shape=jax.ShapeDtypeStruct((count, 128), jnp.float32),
        grid_spec=pltpu.PrefetchScalarGridSpec(
            num_scalar_prefetch=1,
            grid=(steps,),
            in_specs=[block, block, pl.BlockSpec(squares.shape, lambda k, *_: (0, 0, 0))],
            out_specs=pl.BlockSpec((count, 128), lambda k, *_: (0, 0)),
            scratch_shapes=[pltpu.VMEM((npairs, nz, 128), jnp.float32), pltpu.VMEM((npairs, 128), jnp.float32)],
        ),
        compiler_params=pltpu.CompilerParams(vmem_limit_bytes=VMEM_LIMIT),
        name="gram",
    )(half, own, other, squares)


def basis_body(entries, half_ref, raw, own_keep, other_keep, own_send, other_send, out, factor, coef):
    step = pl.program_id(0)
    columns = own_keep.shape[1]
    count = 2 * columns
    steps = pl.num_programs(0)

    @pl.when(step == 0)
    def _():
        total = raw[...]
        lanes = lax.broadcasted_iota(jnp.int32, (count, 128), 1)
        rows = lax.broadcasted_iota(jnp.int32, (count, 128), 0)
        scale = jnp.sqrt(total[:, count : count + 1] / entries + 1e-06)
        inverse_scale = 1.0 / scale
        scale_row = jnp.sum(jnp.where(lanes == rows, jnp.broadcast_to(scale, (count, 128)), 0.0), axis=0, keepdims=True)
        scale_row = jnp.where(lanes < count, jnp.broadcast_to(scale_row, (count, 128)), 1.0)
        gram = total / entries / (jnp.broadcast_to(scale, (count, 128)) * scale_row)
        work = jnp.where(lanes < count, gram, jnp.where(lanes == rows + count, 1.0, 0.0))
        for k in range(count):
            pivot = work[k : k + 1]
            root = jnp.sqrt(pivot[:, k : k + 1])
            line = pivot / root
            ratio = jnp.where(rows[:, 0:1] > k, work[:, k : k + 1], 0.0) / root
            work = jnp.where(rows == k, jnp.broadcast_to(line, (count, 128)), work - ratio * line)
        factor[...] = jnp.where(lanes >= rows, work, 0.0)[:, :count]
        first = half_ref[0] == 0
        for j in range(columns):
            row = jnp.where(first, work[j : j + 1], work[columns + j : columns + j + 1])
            for i in range(count):
                lo = (i + columns) % count
                pick = jnp.where(first, row[:, count + i : count + i + 1], row[:, count + lo : count + lo + 1])
                norm = jnp.where(first, inverse_scale[i : i + 1], inverse_scale[lo : lo + 1])
                coef[j * count + i] = jnp.broadcast_to(pick * norm, coef.shape[1:])

    three, _, nx, nz, ny = own_keep.shape
    keep_step = (step // (steps // 2)) == half_ref[0]

    def combine(own, other):
        for comp in range(three):

            def body(x, _):
                cols = [own[comp, i, x] for i in range(columns)] + [other[comp, i, x] for i in range(columns)]
                for j in range(columns):
                    value = coef[j * count] * cols[0]
                    for i in range(1, count):
                        value = value + coef[j * count + i] * cols[i]
                    out[comp, j, x] = value
                return 0

            lax.fori_loop(0, nx, body, 0)

    @pl.when(keep_step)
    def _():
        combine(own_keep, other_keep)

    @pl.when(jnp.logical_not(keep_step))
    def _():
        combine(own_send, other_send)


def run_basis(entries, half, raw, own_keep, other_keep, own_send, other_send):
    three, columns, half_x, nz, ny = own_keep.shape
    per = 2
    count = 2 * columns
    block = (three, columns, half_x // per, nz, ny)

    def keep_map(k, h):
        inside = k // per == h[0]
        return (0, 0, jnp.where(inside, k % per, jnp.where(h[0] == 0, per - 1, 0)), 0, 0)

    def send_map(k, h):
        inside = k // per != h[0]
        return (0, 0, jnp.where(inside, k % per, jnp.where(h[0] == 0, 0, per - 1)), 0, 0)

    keep_spec, send_spec = pl.BlockSpec(block, keep_map), pl.BlockSpec(block, send_map)
    return pl.pallas_call(
        functools.partial(basis_body, entries),
        out_shape=[
            jax.ShapeDtypeStruct((three, columns, 2 * half_x, nz, ny), jnp.float32),
            jax.ShapeDtypeStruct((count, count), jnp.float32),
        ],
        grid_spec=pltpu.PrefetchScalarGridSpec(
            num_scalar_prefetch=1,
            grid=(2 * per,),
            in_specs=[
                pl.BlockSpec((count, 128), lambda k, *_: (0, 0)),
                keep_spec,
                keep_spec,
                send_spec,
                send_spec,
            ],
            out_specs=[
                pl.BlockSpec(block, lambda k, *_: (0, 0, k, 0, 0)),
                pl.BlockSpec((count, count), lambda k, *_: (0, 0)),
            ],
            scratch_shapes=[pltpu.VMEM((columns * count, nz, ny), jnp.float32)],
        ),
        compiler_params=pltpu.CompilerParams(vmem_limit_bytes=VMEM_LIMIT),
        name="basis",
    )(half, raw, own_keep, other_keep, own_send, other_send)


def shift(value, axis, amount):
    count = lax.axis_size(axis)
    return lax.ppermute(value, axis, [(i, (i + amount) % count) for i in range(count)])


def exchange(first_x, last_x, first_z, last_z):
    zlo = shift(last_z, "gz", 1)
    zhi = shift(first_z, "gz", -1)
    xlo = shift(last_x, "gx", 1)
    xhi = shift(first_x, "gx", -1)
    return xlo, xhi, zlo, zhi


def all_sum(value, axes):
    for axis in axes:
        count = lax.axis_size(axis)
        if count & (count - 1):
            value = lax.psum(value, axis)
            continue
        mask = 1
        while mask < count:
            value = value + lax.ppermute(value, axis, [(i, i ^ mask) for i in range(count)])
            mask *= 2
    return value


def shards(forcing, velocity, wall_solve):
    columns, nx, nz, ny = forcing.shape[1:]
    entries = float(3 * nx * lax.axis_size("gx") * nz * lax.axis_size("gz") * ny)
    faces = exchange(forcing[:, :, 0], forcing[:, :, nx - 1], forcing[:, :, :, 0], forcing[:, :, :, nz - 1])
    shear_rate = shear_of(velocity)
    side = step_length * viscosity
    coef = jnp.stack([side - 0.5 * step_length * velocity, side + 0.5 * step_length * velocity, step_length * shear_rate])
    coef = jnp.broadcast_to(coef[:, None, :], (3, nz, ny))
    wall_high = lax.reduce_precision(wall_solve, 8, 7)
    wall_low = wall_solve - wall_high
    wall = jnp.stack([wall_high, wall_low, wall_high.T, wall_low.T]).astype(jnp.bfloat16)
    half = lax.axis_index("sa").astype(jnp.int32).reshape(1)

    q1, *edge = run_stage("forward_first", forcing, forcing, faces, coef, wall)
    q2, s1, squares, *edge = run_stage("forward_last", q1, forcing, exchange(*edge), coef, wall)
    s2, *edge = run_stage("adjoint_first", s1, q2, exchange(*edge), coef, wall)
    keep, send = run_stage("adjoint_last", s2, q2, exchange(*edge), coef, wall, half)
    other_keep = lax.ppermute(send, "sa", [(0, 1), (1, 0)])
    other_send = lax.ppermute(keep, "sa", [(0, 1)])
    raw = run_gram(half, keep, other_keep, squares)
    raw = all_sum(raw, ("gx", "gz", "sa"))
    basis, factor = run_basis(entries, half, raw, keep, other_keep, send, other_send)
    return basis, factor


def solution(mesh):
    return jax.shard_map(
        shards,
        mesh=mesh,
        in_specs=(P(None, "sa", "gx", "gz", None), P(), P()),
        out_specs=(P(None, "sa", "gx", "gz", None), P()),
        check_vma=False,
    )
```

```python
import functools

import jax
import jax.numpy as jnp
from jax import lax
from jax.experimental import pallas as pl
from jax.experimental.pallas import tpu as pltpu
from jax.sharding import PartitionSpec as P


step_length = 0.4
viscosity = 0.2
VMEM_LIMIT = 8 * 1024 * 1024
X_CHUNK = 4


def split_halves(value):
    high = value.astype(jnp.bfloat16)
    low = (value - high.astype(jnp.float32)).astype(jnp.bfloat16)
    return high, low


def wall_product(high, low, wall_ref):
    dot = functools.partial(jnp.dot, preferred_element_type=jnp.float32)
    return dot(low, wall_ref[0]) + dot(high, wall_ref[1]) + dot(high, wall_ref[0])


def side_row(face, comp, x0, count, nz):
    lanes = face.shape[2]
    rows = [
        jnp.concatenate([face[comp, 0, h, pl.ds(x0 + k, nz, stride=0), :] for h in range(lanes)], axis=1)
        for k in range(count)
    ]
    return jnp.stack(rows, axis=0)


def stencil_chunk(cur, comp, x0, edges, zlo, zhi, coef, adjoint, center):
    mid = cur[comp, 0, pl.ds(x0, X_CHUNK)]
    west = jnp.concatenate([edges[0][None], mid[: X_CHUNK - 1]], axis=0)
    east = jnp.concatenate([mid[1:], edges[1][None]], axis=0)
    nz = mid.shape[1]
    rows = lax.broadcasted_iota(jnp.int32, mid.shape, 1)
    south = jnp.where(rows == 0, side_row(zlo, comp, x0, X_CHUNK, nz), pltpu.roll(mid, 1, 1))
    north = jnp.where(rows == nz - 1, side_row(zhi, comp, x0, X_CHUNK, nz), pltpu.roll(mid, nz - 1, 1))
    plus, minus = coef[0][None], coef[1][None]
    if adjoint:
        plus, minus = minus, plus
    value = center * mid + plus * east + minus * west + (north + south)
    if adjoint and comp == 1:
        value = value - coef[2][None] * cur[0, 0, pl.ds(x0, X_CHUNK)]
    if not adjoint and comp == 0:
        value = value - coef[2][None] * cur[1, 0, pl.ds(x0, X_CHUNK)]
    return value


def put_faces(result, comp, lanes_ref, first_x, last_x, first_z, last_z):
    size = result.shape[0]
    nx, nz = first_z.shape[3], first_x.shape[2]
    first_x[comp, 0] = result[:nz]
    last_x[comp, 0] = result[size - nz :]
    for h in range(lanes_ref.shape[0]):
        lanes_ref[h] = result[:, h * 128 : (h + 1) * 128]
        first_z[comp, 0, h] = lanes_ref[h, pl.ds(0, nx, stride=nz), :]
        last_z[comp, 0, h] = lanes_ref[h, pl.ds(nz - 1, nx, stride=nz), :]


def stage_body(kind, span, *refs):
    half_ref, *refs = refs
    src = None
    if kind == "forward_first":
        cur, *refs = refs
    else:
        cur, src, *refs = refs
    xlo, xhi, zlo, zhi, coef, wall, *rest = refs

    def one(j, _):
        view = lambda ref: ref.at[:, pl.ds(j, 1)]
        fields = [view(cur), None if src is None else view(src), view(xlo), view(xhi), view(zlo), view(zhi), coef, wall]
        if kind == "adjoint_last":
            last_column(half_ref, *fields[:7], *[r.at[:, pl.ds(j - span[0], 1)] for r in rest])
        elif kind == "forward_last":
            out, solved, squares, *more = rest
            faces, work = more[:4], more[4:]
            outs = [view(out), view(solved), squares.at[pl.ds(j, 1)]] + [view(r) for r in faces]
            stage_column(kind, *fields, outs, *work)
        else:
            stage_column(kind, *fields, [view(r) for r in rest[:5]], *rest[5:])
        return 0

    lax.fori_loop(span[0], span[1], one, 0)


def last_column(half_ref, cur, src, xlo, xhi, zlo, zhi, coef, keep, send):
    nx = cur.shape[2]
    half_x = nx // 2
    center = 1.0 / (step_length * viscosity) - 4.0
    for role, target in ((half_ref[0], keep), (1 - half_ref[0], send)):
        base = pl.multiple_of(role * half_x, half_x)
        for comp in range(3):
            for spot in range(0, half_x, X_CHUNK):
                x0 = base + spot
                if spot == 0:
                    west = jnp.where(role == 0, xlo[comp, 0], cur[comp, 0, jnp.maximum(x0 - 1, 0)])
                else:
                    west = cur[comp, 0, x0 - 1]
                if spot + X_CHUNK == half_x:
                    east = jnp.where(role == 1, xhi[comp, 0], cur[comp, 0, jnp.minimum(x0 + X_CHUNK, nx - 1)])
                else:
                    east = cur[comp, 0, x0 + X_CHUNK]
                value = stencil_chunk(cur, comp, x0, (west, east), zlo, zhi, coef, True, center)
                target[comp, 0, spot : spot + X_CHUNK] = value + src[comp, 0, pl.ds(x0, X_CHUNK)]


def stage_column(kind, cur, src, xlo, xhi, zlo, zhi, coef, wall, outs, high, low, lanes):
    nx, nz, ny = cur.shape[2:]
    adjoint = kind.startswith("adjoint")
    center = 1.0 / (step_length * viscosity) - 4.0
    if kind == "forward_first":
        center = center + 1.0 / viscosity
    size = nx * nz
    total = None
    for comp in range(3):
        for x0 in range(0, nx, X_CHUNK):
            west = xlo[comp, 0] if x0 == 0 else cur[comp, 0, x0 - 1]
            east = xhi[comp, 0] if x0 + X_CHUNK == nx else cur[comp, 0, x0 + X_CHUNK]
            value = stencil_chunk(cur, comp, x0, (west, east), zlo, zhi, coef, adjoint, center)
            if kind == "forward_last":
                value = value + (1.0 / viscosity) * src[comp, 0, x0 : x0 + X_CHUNK]
            elif adjoint:
                value = value + src[comp, 0, x0 : x0 + X_CHUNK]
            h, l = split_halves(value.reshape(X_CHUNK * nz, ny))
            spot = (comp * nx + x0) * nz
            high[spot : spot + X_CHUNK * nz] = h
            low[spot : spot + X_CHUNK * nz] = l
        part = slice(comp * size, (comp + 1) * size)
        result = wall_product(high[part], low[part], wall.at[pl.ds(2, 2)] if adjoint else wall.at[pl.ds(0, 2)])
        if kind == "forward_last":
            tile = result.reshape(nx, nz, ny)
            sums = jnp.sum(tile * tile, axis=0)
            total = sums if total is None else total + sums
            scaled = result * (1.0 / viscosity)
            outs[0][comp, 0] = scaled.reshape(nx, nz, ny)
            h, l = split_halves(scaled)
            result = wall_product(h, l, wall.at[pl.ds(4, 2)])
            outs[1][comp, 0] = result.reshape(nx, nz, ny)
        else:
            outs[0][comp, 0] = result.reshape(nx, nz, ny)
        put_faces(result, comp, lanes, *outs[-4:])
    if kind == "forward_last":
        outs[2][0] = total


def in_vmem(shape):
    return pltpu.VMEM(shape, jnp.float32)


def hold(value):
    return pltpu.with_memory_space_constraint(value, pltpu.VMEM)


def run_stage(kind, half, cur, src, faces, coef, wall, span=None):
    three, columns, nx, nz, ny = cur.shape
    span = span or (0, columns)
    field = in_vmem(cur.shape)
    half_field = in_vmem((three, span[1] - span[0], nx // 2, nz, ny))
    x_out = in_vmem((three, columns, nz, ny))
    z_out = in_vmem((three, columns, ny // 128, nx, 128))
    face_outs = [x_out, x_out, z_out, z_out]
    scratch = [pltpu.VMEM((three * nx * nz, ny), jnp.bfloat16)] * 2
    scratch += [pltpu.VMEM((ny // 128, nx * nz, 128), jnp.float32)]
    if kind == "forward_last":
        outs = [field, field, in_vmem((columns, nz, ny))] + face_outs
    elif kind == "adjoint_last":
        outs, scratch = [half_field, half_field], []
    else:
        outs = [field] + face_outs
    fields = (cur,) if src is None else (cur, src)
    operands = [half] + [hold(v) for v in (*fields, *faces, coef, wall)]
    vmem = pl.BlockSpec(memory_space=pltpu.VMEM)
    return pl.pallas_call(
        functools.partial(stage_body, kind, span),
        out_shape=outs,
        in_specs=[pl.BlockSpec(memory_space=pltpu.SMEM)] + [vmem] * (len(operands) - 1),
        out_specs=[vmem] * len(outs),
        scratch_shapes=scratch,
        compiler_params=pltpu.CompilerParams(vmem_limit_bytes=VMEM_LIMIT),
    )(*operands)


def setup_body(wall_solve, velocity, coef, wall):
    ny = wall_solve.shape[0]
    speed = velocity[...]
    lanes = lax.broadcasted_iota(jnp.int32, (1, ny), 1)
    after, before = pltpu.roll(speed, ny - 1, 1), pltpu.roll(speed, 1, 1)
    shear = (after - before) * 0.5
    shear = jnp.where(lanes == 0, after - speed, jnp.where(lanes == ny - 1, speed - before, shear))
    advect = (0.5 / viscosity) * speed
    for k, row in enumerate((1.0 - advect, 1.0 + advect, (1.0 / viscosity) * shear)):
        coef[k] = jnp.broadcast_to(row, coef.shape[1:])
    plain = wall_solve[...]
    turned = plain.T
    for k, value in enumerate((step_length * viscosity * plain, step_length * viscosity * turned, viscosity * turned)):
        wall[2 * k], wall[2 * k + 1] = split_halves(value)


def run_setup(wall_solve, velocity, nz):
    ny = wall_solve.shape[0]
    vmem = pl.BlockSpec(memory_space=pltpu.VMEM)
    return pl.pallas_call(
        setup_body,
        out_shape=[in_vmem((3, nz, ny)), pltpu.VMEM((6, ny, ny), jnp.bfloat16)],
        in_specs=[vmem] * 2,
        out_specs=[vmem] * 2,
        compiler_params=pltpu.CompilerParams(vmem_limit_bytes=VMEM_LIMIT),
        name="setup",
    )(wall_solve, velocity.reshape(1, ny))


def edges_body(source, *refs):
    *outs, lanes, sems = refs
    field, first_x, last_x, first_z, last_z = outs[:5]
    three, columns, nx, nz, ny = field.shape

    def fetch(j):
        return pltpu.make_async_copy(source.at[:, j], field.at[:, j], sems.at[j])

    for j in range(columns):
        fetch(j).start()
    for j in range(columns):
        fetch(j).wait()
        view = lambda ref: ref.at[:, pl.ds(j, 1)]
        for comp in range(three):
            tile = field[comp, j].reshape(nx * nz, ny)
            put_faces(tile, comp, lanes, view(first_x), view(last_x), view(first_z), view(last_z))
            if len(outs) > 5 and j < outs[5].shape[1]:
                outs[5][comp, j] = field[comp, j]


def run_edges(source, front=None):
    three, columns, nx, nz, ny = source.shape
    x_out = in_vmem((three, columns, nz, ny))
    z_out = in_vmem((three, columns, ny // 128, nx, 128))
    outs = [in_vmem(source.shape), x_out, x_out, z_out, z_out]
    if front is not None:
        outs += [in_vmem((three, front, nx, nz, ny))]
    vmem = pl.BlockSpec(memory_space=pltpu.VMEM)
    return pl.pallas_call(
        edges_body,
        out_shape=outs,
        in_specs=[pl.BlockSpec(memory_space=pltpu.HBM)],
        out_specs=[vmem] * len(outs),
        scratch_shapes=[pltpu.VMEM((ny // 128, nx * nz, 128), jnp.float32), pltpu.SemaphoreType.DMA((columns,))],
        compiler_params=pltpu.CompilerParams(vmem_limit_bytes=VMEM_LIMIT),
        name="edges",
    )(pltpu.with_memory_space_constraint(source, pltpu.HBM))


def rows_to_matrix(sums, table, count, columns):
    lanes = lax.broadcasted_iota(jnp.int32, (count, 128), 1)
    zero = jnp.zeros((1, 128), jnp.float32)
    plain = jnp.zeros((count, 128), jnp.float32)
    moved = plain
    for i in range(count):
        if not any((i, j) in table for j in range(count)):
            continue
        stack = jnp.concatenate(
            [sums[table[i, j] : table[i, j] + 1] if (i, j) in table else zero for j in range(count)], axis=0
        )
        column = jnp.sum(stack, axis=1, keepdims=True)
        plain = jnp.where(lanes == i, column, plain)
        moved = jnp.where(lanes == (i + columns) % count, column, moved)
    return plain, moved


def pick_order(plain, moved, half_ref, columns):
    return jnp.where(half_ref[0] == 0, plain, pltpu.roll(moved, columns, 0))


def pair_sums(fields, pairs, acc, nx, three, ny):
    used = sorted({i for pair in pairs for i in pair})
    for lane in range(0, ny, 128):

        def body(k, carry):
            comp = k // nx
            x = k - comp * nx
            cols = {i: fields[i][0][comp, fields[i][1], x, :, lane : lane + 128] for i in used}
            return tuple(c + cols[i] * cols[j] for c, (i, j) in zip(carry, pairs))

        done = lax.fori_loop(0, three * nx, body, tuple(acc[p] for p in range(len(pairs))), unroll=4)
        for p in range(len(pairs)):
            acc[p] = done[p]


def gram_tables(sums, acc, pairs):
    table = {}
    for p, (i, j) in enumerate(pairs):
        sums[p : p + 1] = jnp.sum(acc[p], axis=0, keepdims=True)
        table[i, j] = table[j, i] = p
    return table


def own_gram_body(half_ref, front_keep, front_send, late_keep, late_send, squares, out, acc, sums):
    three, front, nx, _, ny = front_keep.shape
    columns = front + late_keep.shape[1]
    count = 2 * columns
    pairs = [(i, j) for i in range(columns) for j in range(i, columns)]
    acc[...] = jnp.zeros_like(acc)
    for ahead, behind in ((front_keep, late_keep), (front_send, late_send)):
        fields = [(ahead, i) for i in range(front)] + [(behind, i) for i in range(columns - front)]
        pair_sums(fields, pairs, acc, nx, three, ny)
    plain, moved = rows_to_matrix(sums, gram_tables(sums, acc, pairs), count, columns)
    lanes = lax.broadcasted_iota(jnp.int32, (count, 128), 1)
    norm_rows = []
    for i in range(columns):
        rows = sum(squares[i, :, k : k + 128] for k in range(0, ny, 128))
        norm_rows.append(jnp.sum(rows, axis=0, keepdims=True))
    norm_rows += [jnp.zeros((1, 128), jnp.float32)] * columns
    norm = jnp.sum(jnp.concatenate(norm_rows, axis=0), axis=1, keepdims=True)
    plain = jnp.where(lanes == count, norm, plain)
    moved = jnp.where(lanes == count, norm, moved)
    out[...] = pick_order(plain, moved, half_ref, columns)


def cross_gram_body(half_ref, fk, fs, lk, ls, ek, es, other, base, out, acc, sums):
    three, front, nx, _, ny = fk.shape
    late = lk.shape[1]
    columns = front + late
    early = ek.shape[1]
    count = 2 * columns
    wide = [(i, columns + j) for i in range(columns) for j in range(early)]
    narrow = [(front + i, columns + early + j) for i in range(late) for j in range(columns - early)]
    acc[...] = jnp.zeros_like(acc)

    def own(ahead, behind):
        return [(ahead, i) for i in range(front)] + [(behind, i) for i in range(late)]

    for ahead, behind, extra in ((fk, lk, ek), (fs, ls, es)):
        pair_sums(own(ahead, behind) + [(extra, j) for j in range(early)], wide, acc, nx, three, ny)
    rest = acc.at[pl.ds(len(wide), len(narrow))]
    pair_sums(own(fk, lk) + [None] * early + [(other, j) for j in range(columns - early)], narrow, rest, nx, three, ny)
    for p, (i, j) in enumerate(wide):
        if i < early:
            acc[p] = jnp.where(half_ref[0] == 0, acc[p], 0.0)
    plain, moved = rows_to_matrix(sums, gram_tables(sums, acc, wide + narrow), count, columns)
    out[...] = base[...] + pick_order(plain, moved, half_ref, columns)


def run_gram(body, half, fields, npairs, count):
    nz = fields[0].shape[3]
    vmem = pl.BlockSpec(memory_space=pltpu.VMEM)
    return pl.pallas_call(
        body,
        out_shape=jax.ShapeDtypeStruct((count, 128), jnp.float32),
        in_specs=[pl.BlockSpec(memory_space=pltpu.SMEM)] + [vmem] * len(fields),
        out_specs=vmem,
        scratch_shapes=[pltpu.VMEM((npairs, nz, 128), jnp.float32), pltpu.VMEM((npairs, 128), jnp.float32)],
        compiler_params=pltpu.CompilerParams(vmem_limit_bytes=VMEM_LIMIT),
    )(half, *[hold(v) for v in fields])


def factor_body(entries, columns, half_ref, raw, factor, coef):
    side = step_length * viscosity
    count = 2 * columns
    total = raw[...]
    lanes = lax.broadcasted_iota(jnp.int32, (count, 128), 1)
    rows = lax.broadcasted_iota(jnp.int32, (count, 128), 0)
    scale = jnp.sqrt(total[:, count : count + 1] / entries + 1e-06)
    inverse_scale = side / scale
    scale_row = jnp.sum(jnp.where(lanes == rows, jnp.broadcast_to(scale, (count, 128)), 0.0), axis=0, keepdims=True)
    scale_row = jnp.where(lanes < count, jnp.broadcast_to(scale_row, (count, 128)), 1.0)
    gram = total * (side * side / entries) / (jnp.broadcast_to(scale, (count, 128)) * scale_row)
    work = jnp.where(lanes < count, gram, jnp.where(lanes == rows + count, 1.0, 0.0))
    for k in range(count):
        pivot = work[k : k + 1]
        root = jnp.sqrt(pivot[:, k : k + 1])
        line = pivot / root
        ratio = jnp.where(rows[:, 0:1] > k, work[:, k : k + 1], 0.0) / root
        work = jnp.where(rows == k, jnp.broadcast_to(line, (count, 128)), work - ratio * line)
    factor[...] = jnp.where(lanes >= rows, work, 0.0)[:, :count]
    first = half_ref[0] == 0
    for j in range(columns):
        row = jnp.where(first, work[j : j + 1], work[columns + j : columns + j + 1])
        for i in range(count):
            lo = (i + columns) % count
            pick = jnp.where(first, row[:, count + i : count + i + 1], row[:, count + lo : count + lo + 1])
            norm = jnp.where(first, inverse_scale[i : i + 1], inverse_scale[lo : lo + 1])
            coef[j * count + i] = jnp.broadcast_to(pick * norm, coef.shape[1:])


def run_factor(entries, columns, half, raw):
    count = 2 * columns
    vmem = pl.BlockSpec(memory_space=pltpu.VMEM)
    return pl.pallas_call(
        functools.partial(factor_body, entries, columns),
        out_shape=[
            jax.ShapeDtypeStruct((count, count), jnp.float32),
            jax.ShapeDtypeStruct((columns * count, 8, 128), jnp.float32),
        ],
        in_specs=[pl.BlockSpec(memory_space=pltpu.SMEM), vmem],
        out_specs=[vmem, vmem],
        compiler_params=pltpu.CompilerParams(vmem_limit_bytes=VMEM_LIMIT),
        name="factor",
    )(half, raw)


def basis_body(count, aliased, half_ref, coef, *refs):
    fields, out = (refs[:-2], refs[-1]) if aliased else (refs[:-1], refs[-1])
    three, columns, nx, _, ny = out.shape
    base = pl.program_id(0) * nx
    spots = [(ref, i) for ref in fields for i in range(ref.shape[1])]

    def body(k, _):
        comp = k // nx
        x = k - comp * nx
        for lane in range(0, ny, 128):
            part = slice(lane, lane + 128)
            cols = [ref[comp, i, base + x, :, part] for ref, i in spots]
            for j in range(columns):
                terms = [coef[j * count + i] * cols[i] for i in range(count)]
                while len(terms) > 1:
                    terms = [a + b for a, b in zip(terms[::2], terms[1::2])]
                out[comp, j, x, :, part] = terms[0]
        return 0

    lax.fori_loop(0, three * nx, body, 0, unroll=2)


def run_basis(half, coef, fields, columns, keep, target=None):
    three, _, half_x, nz, ny = fields[0].shape
    per = 2
    block = (three, columns, half_x // per, nz, ny)
    vmem = pl.BlockSpec(memory_space=pltpu.VMEM)

    def place(k, h):
        return (0, 0, k + per * (h[0] if keep else 1 - h[0]), 0, 0)

    operands = [hold(v) for v in (coef, *fields)]
    specs = [vmem] * len(operands)
    if target is not None:
        operands, specs = operands + [target], specs + [pl.BlockSpec(memory_space=pl.ANY)]
    return pl.pallas_call(
        functools.partial(basis_body, 2 * columns, target is not None),
        out_shape=jax.ShapeDtypeStruct((three, columns, 2 * half_x, nz, ny), jnp.float32),
        grid_spec=pltpu.PrefetchScalarGridSpec(
            num_scalar_prefetch=1, grid=(per,), in_specs=specs, out_specs=pl.BlockSpec(block, place)
        ),
        input_output_aliases={} if target is None else {len(operands): 0},
        compiler_params=pltpu.CompilerParams(vmem_limit_bytes=VMEM_LIMIT),
        name="basis",
    )(half, *operands)


def shift(value, axis, amount):
    count = lax.axis_size(axis)
    return lax.ppermute(value, axis, [(i, (i + amount) % count) for i in range(count)])


def exchange(first_x, last_x, first_z, last_z):
    zlo = shift(last_z, "gz", 1)
    zhi = shift(first_z, "gz", -1)
    xlo = shift(last_x, "gx", 1)
    xhi = shift(first_x, "gx", -1)
    return xlo, xhi, zlo, zhi


def all_sum(value, axes):
    for axis in axes:
        count = lax.axis_size(axis)
        if count & (count - 1):
            value = lax.psum(value, axis)
            continue
        mask = 1
        while mask < count:
            value = value + lax.ppermute(value, axis, [(i, i ^ mask) for i in range(count)])
            mask *= 2
    return value


def swap(value):
    return lax.ppermute(value, "sa", [(0, 1), (1, 0)])


def shards(forcing, velocity, wall_solve):
    columns, nx, nz, ny = forcing.shape[1:]
    entries = float(3 * nx * lax.axis_size("gx") * nz * lax.axis_size("gz") * ny)
    half = lax.axis_index("sa").astype(jnp.int32).reshape(1)
    early = columns // 2
    count = 2 * columns
    forcing, *edge, front = run_edges(forcing, early)
    guest = swap(front)
    faces = exchange(*edge)
    coef, wall = run_setup(wall_solve, velocity, nz)

    def stage(kind, *args):
        return run_stage(kind, half, *args)

    q1, *edge = stage("forward_first", forcing, None, faces, coef, wall)
    faces = exchange(*edge)
    q2, s1, squares, *edge = stage("forward_last", q1, forcing, faces, coef, wall)
    faces = exchange(*edge)
    s2, *edge = stage("adjoint_first", s1, q2, faces, coef, wall)
    faces = exchange(*edge)
    late_keep, late_send = stage("adjoint_last", s2, q2, faces, coef, wall, (early, columns))
    other_keep = swap(late_send)
    front_keep, front_send = stage("adjoint_last", s2, q2, faces, coef, wall, (0, early))

    guest, *edge = run_edges(guest)
    faces = exchange(*edge)
    g1, *edge = stage("forward_first", guest, None, faces, coef, wall)
    faces = exchange(*edge)
    g2, h1, _, *edge = stage("forward_last", g1, guest, faces, coef, wall)
    faces = exchange(*edge)
    h2, *edge = stage("adjoint_first", h1, g2, faces, coef, wall)
    faces = exchange(*edge)
    early_keep, early_send = stage("adjoint_last", h2, g2, faces, coef, wall)

    own = (front_keep, front_send, late_keep, late_send)
    base = run_gram(own_gram_body, half, (*own, squares), columns * (columns + 1) // 2, count)
    late_keep, other_keep = lax.optimization_barrier((late_keep, other_keep))
    other_send = swap(late_keep)
    cross = (*own, early_keep, early_send, other_keep, base)
    npairs = columns * early + (columns - early) ** 2
    raw = run_gram(cross_gram_body, half, cross, npairs, count)
    raw = all_sum(raw, ("gx", "gz", "sa"))
    factor, coef = run_factor(entries, columns, half, raw)
    basis = run_basis(half, coef, (front_keep, late_keep, early_keep, other_keep), columns, True)
    basis = run_basis(half, coef, (front_send, late_send, early_send, other_send), columns, False, basis)
    return basis, factor


def solution(mesh):
    return jax.shard_map(
        shards,
        mesh=mesh,
        in_specs=(P(None, "sa", "gx", "gz", None), P(), P()),
        out_specs=(P(None, "sa", "gx", "gz", None), P()),
        check_vma=False,
    )
```

```python
import functools

import jax
import jax.numpy as jnp
from jax import lax
from jax.experimental import pallas as pl
from jax.experimental.pallas import tpu as pltpu
from jax.sharding import PartitionSpec as P


step_length = 0.4
viscosity = 0.2
VMEM_LIMIT = 8 * 1024 * 1024
X_CHUNK = 4


def split_halves(value):
    high = value.astype(jnp.bfloat16)
    low = (value - high.astype(jnp.float32)).astype(jnp.bfloat16)
    return high, low


def wall_product(high, low, wall_ref):
    dot = functools.partial(jnp.dot, preferred_element_type=jnp.float32)
    return dot(low, wall_ref[0]) + dot(high, wall_ref[1]) + dot(high, wall_ref[0])


def side_row(face, comp, x0, count, nz):
    lanes = face.shape[2]
    rows = [
        jnp.concatenate([face[comp, 0, h, pl.ds(x0 + k, nz, stride=0), :] for h in range(lanes)], axis=1)
        for k in range(count)
    ]
    return jnp.stack(rows, axis=0)


def stencil_chunk(cur, comp, x0, edges, zlo, zhi, coef, adjoint, center):
    mid = cur[comp, 0, pl.ds(x0, X_CHUNK)]
    west = jnp.concatenate([edges[0][None], mid[: X_CHUNK - 1]], axis=0)
    east = jnp.concatenate([mid[1:], edges[1][None]], axis=0)
    nz = mid.shape[1]
    rows = lax.broadcasted_iota(jnp.int32, mid.shape, 1)
    south = jnp.where(rows == 0, side_row(zlo, comp, x0, X_CHUNK, nz), pltpu.roll(mid, 1, 1))
    north = jnp.where(rows == nz - 1, side_row(zhi, comp, x0, X_CHUNK, nz), pltpu.roll(mid, nz - 1, 1))
    plus, minus = coef[0][None], coef[1][None]
    if adjoint:
        plus, minus = minus, plus
    value = center * mid + plus * east + minus * west + (north + south)
    if adjoint and comp == 1:
        value = value - coef[2][None] * cur[0, 0, pl.ds(x0, X_CHUNK)]
    if not adjoint and comp == 0:
        value = value - coef[2][None] * cur[1, 0, pl.ds(x0, X_CHUNK)]
    return value


def put_faces(result, comp, lanes_ref, faces, nz):
    first_z, last_z, *x_faces = faces
    size = result.shape[0]
    nx = size // nz
    if x_faces:
        x_faces[0][comp, 0] = result[:nz]
        x_faces[1][comp, 0] = result[size - nz :]
    for h in range(lanes_ref.shape[0]):
        lanes_ref[h] = result[:, h * 128 : (h + 1) * 128]
        first_z[comp, 0, h] = lanes_ref[h, pl.ds(0, nx, stride=nz), :]
        last_z[comp, 0, h] = lanes_ref[h, pl.ds(nz - 1, nx, stride=nz), :]


def stage_body(kind, span, guest, relayed, *refs):
    if kind == "adjoint_last":
        half_ref, *refs = refs
    src = None
    if kind == "forward_first":
        cur, *refs = refs
    else:
        cur, src, *refs = refs
    if guest:
        both, *refs = refs
        xlo, xhi = both.at[0], both.at[1]
    else:
        xlo, xhi, *refs = refs
    zlo, zhi, coef, wall, *rest = refs
    if relayed:
        relay, *rest = rest
        relay[0] = xlo[:, : relay.shape[2]]
        relay[1] = xhi[:, : relay.shape[2]]

    def one(j, _):
        view = lambda ref: ref.at[:, pl.ds(j, 1)]
        fields = [view(cur), None if src is None else view(src), view(xlo), view(xhi), view(zlo), view(zhi), coef, wall]
        if kind == "adjoint_last":
            last_column(half_ref, *fields[:7], *[r.at[:, pl.ds(j - span[0], 1)] for r in rest])
        else:
            *outs, high, low, lanes = rest
            squares = None
            if len(outs[-1].shape) == 3:
                *outs, squares = outs
                squares = squares.at[pl.ds(j, 1)]
            stage_column(kind, *fields, [view(r) for r in outs], squares, high, low, lanes)
        return 0

    lax.fori_loop(span[0], span[1], one, 0)


def last_column(half_ref, cur, src, xlo, xhi, zlo, zhi, coef, keep, send):
    nx = cur.shape[2]
    half_x = nx // 2
    center = 1.0 / (step_length * viscosity) - 4.0
    for role, target in ((half_ref[0], keep), (1 - half_ref[0], send)):
        base = pl.multiple_of(role * half_x, half_x)
        for comp in range(3):
            for spot in range(0, half_x, X_CHUNK):
                x0 = base + spot
                if spot == 0:
                    west = jnp.where(role == 0, xlo[comp, 0], cur[comp, 0, jnp.maximum(x0 - 1, 0)])
                else:
                    west = cur[comp, 0, x0 - 1]
                if spot + X_CHUNK == half_x:
                    east = jnp.where(role == 1, xhi[comp, 0], cur[comp, 0, jnp.minimum(x0 + X_CHUNK, nx - 1)])
                else:
                    east = cur[comp, 0, x0 + X_CHUNK]
                value = stencil_chunk(cur, comp, x0, (west, east), zlo, zhi, coef, True, center)
                target[comp, 0, spot : spot + X_CHUNK] = value + src[comp, 0, pl.ds(x0, X_CHUNK)]


def stage_column(kind, cur, src, xlo, xhi, zlo, zhi, coef, wall, outs, squares, high, low, lanes):
    nx, nz, ny = cur.shape[2:]
    adjoint = kind.startswith("adjoint")
    center = 1.0 / (step_length * viscosity) - 4.0
    if kind == "forward_first":
        center = center + 1.0 / viscosity
    size = nx * nz
    total = None
    faces = outs[2:] if kind == "forward_last" else outs[1:]
    for comp in range(3):
        for x0 in range(0, nx, X_CHUNK):
            west = xlo[comp, 0] if x0 == 0 else cur[comp, 0, x0 - 1]
            east = xhi[comp, 0] if x0 + X_CHUNK == nx else cur[comp, 0, x0 + X_CHUNK]
            value = stencil_chunk(cur, comp, x0, (west, east), zlo, zhi, coef, adjoint, center)
            if kind == "forward_last":
                value = value + (1.0 / viscosity) * src[comp, 0, x0 : x0 + X_CHUNK]
            elif adjoint:
                value = value + src[comp, 0, x0 : x0 + X_CHUNK]
            h, l = split_halves(value.reshape(X_CHUNK * nz, ny))
            spot = (comp * nx + x0) * nz
            high[spot : spot + X_CHUNK * nz] = h
            low[spot : spot + X_CHUNK * nz] = l
        part = slice(comp * size, (comp + 1) * size)
        result = wall_product(high[part], low[part], wall.at[pl.ds(2, 2)] if adjoint else wall.at[pl.ds(0, 2)])
        if kind == "forward_last":
            if squares is not None:
                tile = result.reshape(nx, nz, ny)
                sums = jnp.sum(tile * tile, axis=0)
                total = sums if total is None else total + sums
            scaled = result * (1.0 / viscosity)
            outs[0][comp, 0] = scaled.reshape(nx, nz, ny)
            h, l = split_halves(scaled)
            result = wall_product(h, l, wall.at[pl.ds(4, 2)])
            outs[1][comp, 0] = result.reshape(nx, nz, ny)
        else:
            outs[0][comp, 0] = result.reshape(nx, nz, ny)
        put_faces(result, comp, lanes, faces, nz)
    if total is not None:
        squares[0] = total


def in_vmem(shape):
    return pltpu.VMEM(shape, jnp.float32)


def hold(value):
    return pltpu.with_memory_space_constraint(value, pltpu.VMEM)


def run_stage(kind, half, cur, src, faces, coef, wall, span=None, squares=False, relay=0):
    three, columns, nx, nz, ny = cur.shape
    span = span or (0, columns)
    guest = len(faces) == 3
    field = in_vmem(cur.shape)
    half_field = in_vmem((three, span[1] - span[0], nx // 2, nz, ny))
    x_out = in_vmem((three, columns, nz, ny))
    z_out = in_vmem((three, columns, ny // 128, nx, 128))
    face_outs = [z_out, z_out] + ([] if guest else [x_out, x_out])
    scratch = [pltpu.VMEM((three * nx * nz, ny), jnp.bfloat16)] * 2
    scratch += [pltpu.VMEM((ny // 128, nx * nz, 128), jnp.float32)]
    outs = [in_vmem((2, three, relay, nz, ny))] if relay else []
    if kind == "forward_last":
        outs += [field, field] + face_outs + [in_vmem((columns, nz, ny))] * squares
    elif kind == "adjoint_last":
        outs, scratch = outs + [half_field, half_field], []
    else:
        outs += [field] + face_outs
    fields = (cur,) if src is None else (cur, src)
    operands = [hold(v) for v in (*fields, *faces[2:], *faces[:2], coef, wall)]
    vmem = pl.BlockSpec(memory_space=pltpu.VMEM)
    in_specs = [vmem] * len(operands)
    if kind == "adjoint_last":
        operands, in_specs = [half] + operands, [pl.BlockSpec(memory_space=pltpu.SMEM)] + in_specs
    return pl.pallas_call(
        functools.partial(stage_body, kind, span, guest, bool(relay)),
        out_shape=outs,
        in_specs=in_specs,
        out_specs=[vmem] * len(outs),
        scratch_shapes=scratch,
        compiler_params=pltpu.CompilerParams(vmem_limit_bytes=VMEM_LIMIT),
    )(*operands)


def setup_body(wall_solve, velocity, coef, wall):
    ny = wall_solve.shape[0]
    speed = velocity[...]
    lanes = lax.broadcasted_iota(jnp.int32, (1, ny), 1)
    after, before = pltpu.roll(speed, ny - 1, 1), pltpu.roll(speed, 1, 1)
    shear = (after - before) * 0.5
    shear = jnp.where(lanes == 0, after - speed, jnp.where(lanes == ny - 1, speed - before, shear))
    advect = (0.5 / viscosity) * speed
    for k, row in enumerate((1.0 - advect, 1.0 + advect, (1.0 / viscosity) * shear)):
        coef[k] = jnp.broadcast_to(row, coef.shape[1:])
    plain = wall_solve[...]
    turned = plain.T
    for k, value in enumerate((step_length * viscosity * plain, step_length * viscosity * turned, viscosity * turned)):
        wall[2 * k], wall[2 * k + 1] = split_halves(value)


def run_setup(wall_solve, velocity, nz):
    ny = wall_solve.shape[0]
    vmem = pl.BlockSpec(memory_space=pltpu.VMEM)
    return pl.pallas_call(
        setup_body,
        out_shape=[in_vmem((3, nz, ny)), pltpu.VMEM((6, ny, ny), jnp.bfloat16)],
        in_specs=[vmem] * 2,
        out_specs=[vmem] * 2,
        compiler_params=pltpu.CompilerParams(vmem_limit_bytes=VMEM_LIMIT),
        name="setup",
    )(wall_solve, velocity.reshape(1, ny))


def edges_body(source, half_ref, field, front, first_z, last_z, first_x, last_x, lanes, sems):
    three, columns, nx, nz, ny = field.shape

    def fetch(j):
        return pltpu.make_async_copy(source.at[:, j], field.at[:, j], sems.at[j])

    for j in range(columns):
        fetch(j).start()
    ahead = pltpu.make_async_copy(source.at[:, pl.ds(0, front.shape[1])], front, sems.at[columns])
    ahead.start()
    for j in range(columns):
        fetch(j).wait()
        faces = [ref.at[:, pl.ds(j, 1)] for ref in (first_z, last_z, first_x, last_x)]
        for comp in range(three):
            put_faces(field[comp, j].reshape(nx * nz, ny), comp, lanes, faces, nz)
    ahead.wait()


def run_edges(source, half, front):
    three, columns, nx, nz, ny = source.shape
    x_out = in_vmem((three, columns, nz, ny))
    z_out = in_vmem((three, columns, ny // 128, nx, 128))
    outs = [in_vmem(source.shape), in_vmem((three, front, nx, nz, ny)), z_out, z_out, x_out, x_out]
    return pl.pallas_call(
        edges_body,
        out_shape=outs,
        in_specs=[pl.BlockSpec(memory_space=pltpu.HBM), pl.BlockSpec(memory_space=pltpu.SMEM)],
        out_specs=[pl.BlockSpec(memory_space=pltpu.VMEM)] * len(outs),
        scratch_shapes=[pltpu.VMEM((ny // 128, nx * nz, 128), jnp.float32), pltpu.SemaphoreType.DMA((columns + 1,))],
        compiler_params=pltpu.CompilerParams(vmem_limit_bytes=VMEM_LIMIT),
        name="edges",
    )(pltpu.with_memory_space_constraint(source, pltpu.HBM), half)


def guest_edges_body(field, first_z, last_z, lanes):
    three, columns, nx, nz, ny = field.shape
    for j in range(columns):
        faces = [ref.at[:, pl.ds(j, 1)] for ref in (first_z, last_z)]
        for comp in range(three):
            put_faces(field[comp, j].reshape(nx * nz, ny), comp, lanes, faces, nz)


def run_guest_edges(field):
    three, columns, nx, nz, ny = field.shape
    z_out = in_vmem((three, columns, ny // 128, nx, 128))
    vmem = pl.BlockSpec(memory_space=pltpu.VMEM)
    return pl.pallas_call(
        guest_edges_body,
        out_shape=[z_out, z_out],
        in_specs=[vmem],
        out_specs=[vmem] * 2,
        scratch_shapes=[pltpu.VMEM((ny // 128, nx * nz, 128), jnp.float32)],
        compiler_params=pltpu.CompilerParams(vmem_limit_bytes=VMEM_LIMIT),
        name="guest_edges",
    )(hold(field))


def rows_to_matrix(sums, table, count, columns):
    lanes = lax.broadcasted_iota(jnp.int32, (count, 128), 1)
    zero = jnp.zeros((1, 128), jnp.float32)
    plain = jnp.zeros((count, 128), jnp.float32)
    moved = plain
    for i in range(count):
        if not any((i, j) in table for j in range(count)):
            continue
        stack = jnp.concatenate(
            [sums[table[i, j] : table[i, j] + 1] if (i, j) in table else zero for j in range(count)], axis=0
        )
        column = jnp.sum(stack, axis=1, keepdims=True)
        plain = jnp.where(lanes == i, column, plain)
        moved = jnp.where(lanes == (i + columns) % count, column, moved)
    return plain, moved


def pick_order(plain, moved, half_ref, columns):
    return jnp.where(half_ref[0] == 0, plain, pltpu.roll(moved, columns, 0))


def pair_sums(fields, pairs, acc, nx, three, ny):
    used = sorted({i for pair in pairs for i in pair})
    total = tuple(acc[p] for p in range(len(pairs)))
    for comp in range(three):

        def body(x, carry):
            for lane in range(0, ny, 128):
                cols = {i: fields[i][0][comp, fields[i][1], x, :, lane : lane + 128] for i in used}
                carry = tuple(c + cols[i] * cols[j] for c, (i, j) in zip(carry, pairs))
            return carry

        total = lax.fori_loop(0, nx, body, total, unroll=4)
    for p in range(len(pairs)):
        acc[p] = total[p]


def gram_tables(sums, acc, pairs):
    table = {}
    for p, (i, j) in enumerate(pairs):
        sums[p : p + 1] = jnp.sum(acc[p], axis=0, keepdims=True)
        table[i, j] = table[j, i] = p
    return table


def own_gram_body(half_ref, front_keep, front_send, late_keep, late_send, squares, out, acc, sums):
    three, front, nx, _, ny = front_keep.shape
    columns = front + late_keep.shape[1]
    count = 2 * columns
    pairs = [(i, j) for i in range(columns) for j in range(i, columns)]
    acc[...] = jnp.zeros_like(acc)
    for ahead, behind in ((front_keep, late_keep), (front_send, late_send)):
        fields = [(ahead, i) for i in range(front)] + [(behind, i) for i in range(columns - front)]
        pair_sums(fields, pairs, acc, nx, three, ny)
    plain, moved = rows_to_matrix(sums, gram_tables(sums, acc, pairs), count, columns)
    lanes = lax.broadcasted_iota(jnp.int32, (count, 128), 1)
    norm_rows = []
    for i in range(columns):
        rows = sum(squares[i, :, k : k + 128] for k in range(0, ny, 128))
        norm_rows.append(jnp.sum(rows, axis=0, keepdims=True))
    norm_rows += [jnp.zeros((1, 128), jnp.float32)] * columns
    norm = jnp.sum(jnp.concatenate(norm_rows, axis=0), axis=1, keepdims=True)
    plain = jnp.where(lanes == count, norm, plain)
    moved = jnp.where(lanes == count, norm, moved)
    out[...] = pick_order(plain, moved, half_ref, columns)


def cross_gram_body(half_ref, fk, fs, lk, ls, ek, es, other, base, out, acc, sums):
    three, front, nx, _, ny = fk.shape
    late = lk.shape[1]
    columns = front + late
    early = ek.shape[1]
    count = 2 * columns
    wide = [(i, columns + j) for i in range(columns) for j in range(early)]
    narrow = [(front + i, columns + early + j) for i in range(late) for j in range(columns - early)]
    acc[...] = jnp.zeros_like(acc)

    def own(ahead, behind):
        return [(ahead, i) for i in range(front)] + [(behind, i) for i in range(late)]

    for ahead, behind, extra in ((fk, lk, ek), (fs, ls, es)):
        pair_sums(own(ahead, behind) + [(extra, j) for j in range(early)], wide, acc, nx, three, ny)
    rest = acc.at[pl.ds(len(wide), len(narrow))]
    pair_sums(own(fk, lk) + [None] * early + [(other, j) for j in range(columns - early)], narrow, rest, nx, three, ny)
    for p, (i, j) in enumerate(wide):
        if i < early:
            acc[p] = jnp.where(half_ref[0] == 0, acc[p], 0.0)
    plain, moved = rows_to_matrix(sums, gram_tables(sums, acc, wide + narrow), count, columns)
    out[...] = base[...] + pick_order(plain, moved, half_ref, columns)


def run_gram(body, half, fields, npairs, count):
    nz = fields[0].shape[3]
    vmem = pl.BlockSpec(memory_space=pltpu.VMEM)
    return pl.pallas_call(
        body,
        out_shape=jax.ShapeDtypeStruct((count, 128), jnp.float32),
        in_specs=[pl.BlockSpec(memory_space=pltpu.SMEM)] + [vmem] * len(fields),
        out_specs=vmem,
        scratch_shapes=[pltpu.VMEM((npairs, nz, 128), jnp.float32), pltpu.VMEM((npairs, 128), jnp.float32)],
        compiler_params=pltpu.CompilerParams(vmem_limit_bytes=VMEM_LIMIT),
    )(half, *[hold(v) for v in fields])


def factor_body(entries, columns, half_ref, raw, factor, coef):
    side = step_length * viscosity
    count = 2 * columns
    total = raw[...]
    lanes = lax.broadcasted_iota(jnp.int32, (count, 128), 1)
    rows = lax.broadcasted_iota(jnp.int32, (count, 128), 0)
    scale = jnp.sqrt(total[:, count : count + 1] / entries + 1e-06)
    inverse_scale = side / scale
    scale_row = jnp.sum(jnp.where(lanes == rows, jnp.broadcast_to(scale, (count, 128)), 0.0), axis=0, keepdims=True)
    scale_row = jnp.where(lanes < count, jnp.broadcast_to(scale_row, (count, 128)), 1.0)
    gram = total * (side * side / entries) / (jnp.broadcast_to(scale, (count, 128)) * scale_row)
    work = jnp.where(lanes < count, gram, jnp.where(lanes == rows + count, 1.0, 0.0))
    for k in range(count):
        pivot = work[k : k + 1]
        root = jnp.sqrt(pivot[:, k : k + 1])
        line = pivot / root
        ratio = jnp.where(rows[:, 0:1] > k, work[:, k : k + 1], 0.0) / root
        work = jnp.where(rows == k, jnp.broadcast_to(line, (count, 128)), work - ratio * line)
    factor[...] = jnp.where(lanes >= rows, work, 0.0)[:, :count]
    first = half_ref[0] == 0
    for j in range(columns):
        row = jnp.where(first, work[j : j + 1], work[columns + j : columns + j + 1])
        for i in range(count):
            lo = (i + columns) % count
            pick = jnp.where(first, row[:, count + i : count + i + 1], row[:, count + lo : count + lo + 1])
            norm = jnp.where(first, inverse_scale[i : i + 1], inverse_scale[lo : lo + 1])
            coef[j * count + i] = jnp.broadcast_to(pick * norm, coef.shape[1:])


def run_factor(entries, columns, half, raw):
    count = 2 * columns
    vmem = pl.BlockSpec(memory_space=pltpu.VMEM)
    return pl.pallas_call(
        functools.partial(factor_body, entries, columns),
        out_shape=[
            jax.ShapeDtypeStruct((count, count), jnp.float32),
            jax.ShapeDtypeStruct((columns * count, 8, 128), jnp.float32),
        ],
        in_specs=[pl.BlockSpec(memory_space=pltpu.SMEM), vmem],
        out_specs=[vmem, vmem],
        compiler_params=pltpu.CompilerParams(vmem_limit_bytes=VMEM_LIMIT),
        name="factor",
    )(half, raw)


def basis_body(count, aliased, half_ref, coef, *refs):
    fields, out = (refs[:-2], refs[-1]) if aliased else (refs[:-1], refs[-1])
    three, columns, nx, _, ny = out.shape
    base = pl.program_id(0) * nx
    spots = [(ref, i) for ref in fields for i in range(ref.shape[1])]

    for comp in range(three):

        def body(x, _):
            for lane in range(0, ny, 128):
                part = slice(lane, lane + 128)
                cols = [ref[comp, i, base + x, :, part] for ref, i in spots]
                for j in range(columns):
                    terms = [coef[j * count + i] * cols[i] for i in range(count)]
                    while len(terms) > 1:
                        terms = [a + b for a, b in zip(terms[::2], terms[1::2])]
                    out[comp, j, x, :, part] = terms[0]
            return 0

        lax.fori_loop(0, nx, body, 0, unroll=4)


def run_basis(half, coef, fields, columns, keep, target=None):
    three, _, half_x, nz, ny = fields[0].shape
    per = 2
    block = (three, columns, half_x // per, nz, ny)
    vmem = pl.BlockSpec(memory_space=pltpu.VMEM)

    def place(k, h):
        return (0, 0, k + per * (h[0] if keep else 1 - h[0]), 0, 0)

    operands = [hold(v) for v in (coef, *fields)]
    specs = [vmem] * len(operands)
    if target is not None:
        operands, specs = operands + [target], specs + [pl.BlockSpec(memory_space=pl.ANY)]
    return pl.pallas_call(
        functools.partial(basis_body, 2 * columns, target is not None),
        out_shape=jax.ShapeDtypeStruct((three, columns, 2 * half_x, nz, ny), jnp.float32),
        grid_spec=pltpu.PrefetchScalarGridSpec(
            num_scalar_prefetch=1, grid=(per,), in_specs=specs, out_specs=pl.BlockSpec(block, place)
        ),
        input_output_aliases={} if target is None else {len(operands): 0},
        compiler_params=pltpu.CompilerParams(vmem_limit_bytes=VMEM_LIMIT),
        name="basis",
    )(half, *operands)


def shift(value, axis, amount):
    count = lax.axis_size(axis)
    return lax.ppermute(value, axis, [(i, (i + amount) % count) for i in range(count)])


def exchange(first_z, last_z, first_x=None, last_x=None):
    zlo = shift(last_z, "gz", 1)
    zhi = shift(first_z, "gz", -1)
    if first_x is None:
        return zlo, zhi
    xlo = shift(last_x, "gx", 1)
    xhi = shift(first_x, "gx", -1)
    return zlo, zhi, xlo, xhi


def partner(value, axis, count, mask):
    return lax.ppermute(value, axis, [(i, i ^ mask) for i in range(count)])


def all_sum(value, axes, wide):
    for axis in axes:
        count = lax.axis_size(axis)
        if count & (count - 1):
            value = lax.psum(value, axis)
            continue
        mask = 1
        while mask < count:
            if wide == axis and 4 * mask <= count:
                near, far, both = (partner(value, axis, count, k * mask) for k in (1, 2, 3))
                value = (value + near) + (far + both)
                mask *= 4
            else:
                value = value + partner(value, axis, count, mask)
                mask *= 2
    return value


def swap(value):
    return lax.ppermute(value, "sa", [(0, 1), (1, 0)])


def shards(forcing, velocity, wall_solve):
    columns, nx, nz, ny = forcing.shape[1:]
    entries = float(3 * nx * lax.axis_size("gx") * nz * lax.axis_size("gz") * ny)
    half = lax.axis_index("sa").astype(jnp.int32).reshape(1)
    early = columns // 2
    count = 2 * columns
    forcing, front, *edge = run_edges(forcing, half, early)
    guest = swap(front)
    faces = exchange(*edge)
    coef, wall = run_setup(wall_solve, velocity, nz)

    def stage(kind, *args, **kwargs):
        return run_stage(kind, half, *args, **kwargs)

    relay, q1, *edge = stage("forward_first", forcing, None, faces, coef, wall, relay=early)
    faces = exchange(*edge)
    side1 = swap(relay)
    relay, q2, s1, *edge, squares = stage("forward_last", q1, forcing, faces, coef, wall, squares=True, relay=early)
    faces = exchange(*edge)
    side2 = swap(relay)
    relay, s2, *edge = stage("adjoint_first", s1, q2, faces, coef, wall, relay=early)
    faces = exchange(*edge)
    side3 = swap(relay)
    relay, late_keep, late_send = stage("adjoint_last", s2, q2, faces, coef, wall, span=(early, columns), relay=early)
    side4 = swap(relay)
    other_keep = swap(late_send)
    front_keep, front_send = stage("adjoint_last", s2, q2, faces, coef, wall, span=(0, early))

    edge = run_guest_edges(guest)
    faces = exchange(*edge)
    g1, *edge = stage("forward_first", guest, None, (*faces, side1), coef, wall)
    faces = exchange(*edge)
    g2, h1, *edge = stage("forward_last", g1, guest, (*faces, side2), coef, wall)
    faces = exchange(*edge)
    h2, *edge = stage("adjoint_first", h1, g2, (*faces, side3), coef, wall)
    faces = exchange(*edge)
    early_keep, early_send = stage("adjoint_last", h2, g2, (*faces, side4), coef, wall)

    own = (front_keep, front_send, late_keep, late_send)
    base = run_gram(own_gram_body, half, (*own, squares), columns * (columns + 1) // 2, count)
    late_keep, other_keep = lax.optimization_barrier((late_keep, other_keep))
    other_send = swap(late_keep)
    cross = (*own, early_keep, early_send, other_keep, base)
    npairs = columns * early + (columns - early) ** 2
    raw = run_gram(cross_gram_body, half, cross, npairs, count)
    raw = all_sum(raw, ("sa",), "gz")
    raw = all_sum(raw, ("gx",), "gz")
    raw = all_sum(raw, ("gz",), "gz")
    factor, coef = run_factor(entries, columns, half, raw)
    basis = run_basis(half, coef, (front_keep, late_keep, early_keep, other_keep), columns, True)
    basis = run_basis(half, coef, (front_send, late_send, early_send, other_send), columns, False, basis)
    return basis, factor


def solution(mesh):
    return jax.shard_map(
        shards,
        mesh=mesh,
        in_specs=(P(None, "sa", "gx", "gz", None), P(), P()),
        out_specs=(P(None, "sa", "gx", "gz", None), P()),
        check_vma=False,
    )
```

```python
import functools

import jax
import jax.numpy as jnp
from jax import lax
from jax.experimental import pallas as pl
from jax.experimental.pallas import tpu as pltpu
from jax.sharding import PartitionSpec as P


step_length = 0.4
viscosity = 0.2
VMEM_LIMIT = 8 * 1024 * 1024
X_CHUNK = 4
ROW_PARTS = 2


def split_halves(value):
    high = value.astype(jnp.bfloat16)
    low = (value - high.astype(jnp.float32)).astype(jnp.bfloat16)
    return high, low


def wall_product(high, low, wall_ref):
    dot = functools.partial(jnp.dot, preferred_element_type=jnp.float32)
    return dot(low, wall_ref[0]) + dot(high, wall_ref[1]) + dot(high, wall_ref[0])


def side_row(face, comp, x0, count, nz):
    lanes = face.shape[2]
    rows = [
        jnp.concatenate([face[comp, 0, h, pl.ds(x0 + k, nz, stride=0), :] for h in range(lanes)], axis=1)
        for k in range(count)
    ]
    return jnp.stack(rows, axis=0)


def stencil_chunk(cur, comp, x0, edges, zlo, zhi, coef, adjoint, center):
    mid = cur[comp, 0, pl.ds(x0, X_CHUNK)]
    west = jnp.concatenate([edges[0][None], mid[: X_CHUNK - 1]], axis=0)
    east = jnp.concatenate([mid[1:], edges[1][None]], axis=0)
    nz = mid.shape[1]
    rows = lax.broadcasted_iota(jnp.int32, mid.shape, 1)
    south = jnp.where(rows == 0, side_row(zlo, comp, x0, X_CHUNK, nz), pltpu.roll(mid, 1, 1))
    north = jnp.where(rows == nz - 1, side_row(zhi, comp, x0, X_CHUNK, nz), pltpu.roll(mid, nz - 1, 1))
    plus, minus = coef[0][None], coef[1][None]
    if adjoint:
        plus, minus = minus, plus
    value = center * mid + plus * east + minus * west + (north + south)
    if adjoint and comp == 1:
        value = value - coef[2][None] * cur[0, 0, pl.ds(x0, X_CHUNK)]
    if not adjoint and comp == 0:
        value = value - coef[2][None] * cur[1, 0, pl.ds(x0, X_CHUNK)]
    return value


def put_faces(result, comp, lanes_ref, faces, nz, x0=0, nx=None):
    first_z, last_z, *x_faces = faces
    size = result.shape[0]
    step = size // nz
    if x_faces and x0 == 0:
        x_faces[0][comp, 0] = result[:nz]
    if x_faces and x0 + step == (nx or step):
        x_faces[1][comp, 0] = result[size - nz :]
    for h in range(lanes_ref.shape[0]):
        lanes_ref[h, x0 * nz : x0 * nz + size] = result[:, h * 128 : (h + 1) * 128]
        first_z[comp, 0, h, x0 : x0 + step] = lanes_ref[h, pl.ds(x0 * nz, step, stride=nz), :]
        last_z[comp, 0, h, x0 : x0 + step] = lanes_ref[h, pl.ds(x0 * nz + nz - 1, step, stride=nz), :]


def stage_body(kind, span, guest, place, relayed, *refs):
    if kind == "adjoint_last":
        half_ref, *refs = refs
    src = None
    if kind == "forward_first":
        cur, *refs = refs
    else:
        cur, src, *refs = refs
    if guest:
        both, *refs = refs
        xlo, xhi = both.at[2 * place], both.at[2 * place + 1]
    else:
        xlo, xhi, *refs = refs
    zlo, zhi, coef, wall, *rest = refs
    if relayed:
        relay, *rest = rest
        relay[0] = xlo[:, : relay.shape[2]]
        relay[1] = xhi[:, : relay.shape[2]]

    def one(j, _):
        view = lambda ref: ref.at[:, pl.ds(j, 1)]
        fields = [view(cur), None if src is None else view(src), view(xlo), view(xhi), view(zlo), view(zhi), coef, wall]
        if kind == "adjoint_last":
            last_column(half_ref, *fields[:7], *[r.at[:, pl.ds(j - span[0], 1)] for r in rest])
        else:
            *outs, high, low, lanes = rest
            squares = None
            if len(outs[-1].shape) == 3:
                *outs, squares = outs
                squares = squares.at[pl.ds(j, 1)]
            stage_column(kind, *fields, [view(r) for r in outs], squares, high, low, lanes)
        return 0

    lax.fori_loop(span[0], span[1], one, 0)


def last_column(half_ref, cur, src, xlo, xhi, zlo, zhi, coef, keep, send):
    nx = cur.shape[2]
    half_x = nx // 2
    center = 1.0 / (step_length * viscosity) - 4.0
    for role, target in ((half_ref[0], keep), (1 - half_ref[0], send)):
        base = pl.multiple_of(role * half_x, half_x)
        for comp in range(3):
            for spot in range(0, half_x, X_CHUNK):
                x0 = base + spot
                if spot == 0:
                    west = jnp.where(role == 0, xlo[comp, 0], cur[comp, 0, jnp.maximum(x0 - 1, 0)])
                else:
                    west = cur[comp, 0, x0 - 1]
                if spot + X_CHUNK == half_x:
                    east = jnp.where(role == 1, xhi[comp, 0], cur[comp, 0, jnp.minimum(x0 + X_CHUNK, nx - 1)])
                else:
                    east = cur[comp, 0, x0 + X_CHUNK]
                value = stencil_chunk(cur, comp, x0, (west, east), zlo, zhi, coef, True, center)
                target[comp, 0, spot : spot + X_CHUNK] = value + src[comp, 0, pl.ds(x0, X_CHUNK)]


def stage_column(kind, cur, src, xlo, xhi, zlo, zhi, coef, wall, outs, squares, high, low, lanes):
    nx, nz, ny = cur.shape[2:]
    adjoint = kind.startswith("adjoint")
    center = 1.0 / (step_length * viscosity) - 4.0
    if kind == "forward_first":
        center = center + 1.0 / viscosity
    total = None
    faces = outs[2:] if kind == "forward_last" else outs[1:]
    for comp in range(3):
        for x0 in range(0, nx, X_CHUNK):
            west = xlo[comp, 0] if x0 == 0 else cur[comp, 0, x0 - 1]
            east = xhi[comp, 0] if x0 + X_CHUNK == nx else cur[comp, 0, x0 + X_CHUNK]
            value = stencil_chunk(cur, comp, x0, (west, east), zlo, zhi, coef, adjoint, center)
            if kind == "forward_last":
                value = value + (1.0 / viscosity) * src[comp, 0, x0 : x0 + X_CHUNK]
            elif adjoint:
                value = value + src[comp, 0, x0 : x0 + X_CHUNK]
            h, l = split_halves(value.reshape(X_CHUNK * nz, ny))
            spot = (comp * nx + x0) * nz
            high[spot : spot + X_CHUNK * nz] = h
            low[spot : spot + X_CHUNK * nz] = l
        step = nx if kind == "forward_last" else nx // ROW_PARTS
        for x0 in range(0, nx, step):
            part = slice((comp * nx + x0) * nz, (comp * nx + x0 + step) * nz)
            result = wall_product(high[part], low[part], wall.at[pl.ds(2, 2)] if adjoint else wall.at[pl.ds(0, 2)])
            if kind == "forward_last":
                if squares is not None:
                    tile = result.reshape(step, nz, ny)
                    sums = jnp.sum(tile * tile, axis=0)
                    total = sums if total is None else total + sums
                scaled = result * (1.0 / viscosity)
                outs[0][comp, 0, x0 : x0 + step] = scaled.reshape(step, nz, ny)
                h, l = split_halves(scaled)
                result = wall_product(h, l, wall.at[pl.ds(4, 2)])
                outs[1][comp, 0, x0 : x0 + step] = result.reshape(step, nz, ny)
            else:
                outs[0][comp, 0, x0 : x0 + step] = result.reshape(step, nz, ny)
            put_faces(result, comp, lanes, faces, nz, x0, nx)
    if total is not None:
        squares[0] = total


def in_vmem(shape):
    return pltpu.VMEM(shape, jnp.float32)


def hold(value):
    return pltpu.with_memory_space_constraint(value, pltpu.VMEM)


def run_stage(kind, half, cur, src, faces, coef, wall, span=None, squares=False, relay=0, place=0):
    three, columns, nx, nz, ny = cur.shape
    span = span or (0, columns)
    guest = len(faces) == 3
    field = in_vmem(cur.shape)
    half_field = in_vmem((three, span[1] - span[0], nx // 2, nz, ny))
    x_out = in_vmem((three, columns, nz, ny))
    z_out = in_vmem((three, columns, ny // 128, nx, 128))
    face_outs = [z_out, z_out] + ([] if guest else [x_out, x_out])
    scratch = [pltpu.VMEM((three * nx * nz, ny), jnp.bfloat16)] * 2
    scratch += [pltpu.VMEM((ny // 128, nx * nz, 128), jnp.float32)]
    outs = [in_vmem((2, three, relay, nz, ny))] if relay else []
    if kind == "forward_last":
        outs += [field, field] + face_outs + [in_vmem((columns, nz, ny))] * squares
    elif kind == "adjoint_last":
        outs, scratch = outs + [half_field, half_field], []
    else:
        outs += [field] + face_outs
    fields = (cur,) if src is None else (cur, src)
    operands = [hold(v) for v in (*fields, *faces[2:], *faces[:2], coef, wall)]
    vmem = pl.BlockSpec(memory_space=pltpu.VMEM)
    in_specs = [vmem] * len(operands)
    if kind == "adjoint_last":
        operands, in_specs = [half] + operands, [pl.BlockSpec(memory_space=pltpu.SMEM)] + in_specs
    return pl.pallas_call(
        functools.partial(stage_body, kind, span, guest, place, bool(relay)),
        out_shape=outs,
        in_specs=in_specs,
        out_specs=[vmem] * len(outs),
        scratch_shapes=scratch,
        compiler_params=pltpu.CompilerParams(vmem_limit_bytes=VMEM_LIMIT),
    )(*operands)


def setup_body(wall_solve, velocity, coef, wall):
    ny = wall_solve.shape[0]
    speed = velocity[...]
    lanes = lax.broadcasted_iota(jnp.int32, (1, ny), 1)
    after, before = pltpu.roll(speed, ny - 1, 1), pltpu.roll(speed, 1, 1)
    shear = (after - before) * 0.5
    shear = jnp.where(lanes == 0, after - speed, jnp.where(lanes == ny - 1, speed - before, shear))
    advect = (0.5 / viscosity) * speed
    for k, row in enumerate((1.0 - advect, 1.0 + advect, (1.0 / viscosity) * shear)):
        coef[k] = jnp.broadcast_to(row, coef.shape[1:])
    plain = wall_solve[...]
    turned = plain.T
    for k, value in enumerate((step_length * viscosity * plain, step_length * viscosity * turned, viscosity * turned)):
        wall[2 * k], wall[2 * k + 1] = split_halves(value)


def run_setup(wall_solve, velocity, nz):
    ny = wall_solve.shape[0]
    vmem = pl.BlockSpec(memory_space=pltpu.VMEM)
    return pl.pallas_call(
        setup_body,
        out_shape=[in_vmem((3, nz, ny)), pltpu.VMEM((6, ny, ny), jnp.bfloat16)],
        in_specs=[vmem] * 2,
        out_specs=[vmem] * 2,
        compiler_params=pltpu.CompilerParams(vmem_limit_bytes=VMEM_LIMIT),
        name="setup",
    )(wall_solve, velocity.reshape(1, ny))


def edges_body(source, half_ref, field, front, first_z, last_z, first_x, last_x, lanes, sems):
    three, columns, nx, nz, ny = field.shape

    def fetch(j):
        return pltpu.make_async_copy(source.at[:, j], field.at[:, j], sems.at[j])

    for j in range(columns):
        fetch(j).start()
    ahead = pltpu.make_async_copy(source.at[:, pl.ds(0, front.shape[1])], front, sems.at[columns])
    ahead.start()
    for j in range(columns):
        fetch(j).wait()
        faces = [ref.at[:, pl.ds(j, 1)] for ref in (first_z, last_z, first_x, last_x)]
        for comp in range(three):
            put_faces(field[comp, j].reshape(nx * nz, ny), comp, lanes, faces, nz)
    ahead.wait()


def run_edges(source, half, front):
    three, columns, nx, nz, ny = source.shape
    x_out = in_vmem((three, columns, nz, ny))
    z_out = in_vmem((three, columns, ny // 128, nx, 128))
    outs = [in_vmem(source.shape), in_vmem((three, front, nx, nz, ny)), z_out, z_out, x_out, x_out]
    return pl.pallas_call(
        edges_body,
        out_shape=outs,
        in_specs=[pl.BlockSpec(memory_space=pltpu.HBM), pl.BlockSpec(memory_space=pltpu.SMEM)],
        out_specs=[pl.BlockSpec(memory_space=pltpu.VMEM)] * len(outs),
        scratch_shapes=[pltpu.VMEM((ny // 128, nx * nz, 128), jnp.float32), pltpu.SemaphoreType.DMA((columns + 1,))],
        compiler_params=pltpu.CompilerParams(vmem_limit_bytes=VMEM_LIMIT),
        name="edges",
    )(pltpu.with_memory_space_constraint(source, pltpu.HBM), half)


def guest_edges_body(field, first_z, last_z, lanes):
    three, columns, nx, nz, ny = field.shape
    for j in range(columns):
        faces = [ref.at[:, pl.ds(j, 1)] for ref in (first_z, last_z)]
        for comp in range(three):
            put_faces(field[comp, j].reshape(nx * nz, ny), comp, lanes, faces, nz)


def relay_body(earlier, xlo, xhi, out):
    out[0], out[1] = earlier[0], earlier[1]
    out[2] = xlo[:, : out.shape[2]]
    out[3] = xhi[:, : out.shape[2]]


def run_relay(earlier, xlo, xhi):
    vmem = pl.BlockSpec(memory_space=pltpu.VMEM)
    return pl.pallas_call(
        relay_body,
        out_shape=in_vmem((4, *earlier.shape[1:])),
        in_specs=[vmem] * 3,
        out_specs=vmem,
        compiler_params=pltpu.CompilerParams(vmem_limit_bytes=VMEM_LIMIT),
        name="relay",
    )(hold(earlier), hold(xlo), hold(xhi))


def run_guest_edges(field):
    three, columns, nx, nz, ny = field.shape
    z_out = in_vmem((three, columns, ny // 128, nx, 128))
    vmem = pl.BlockSpec(memory_space=pltpu.VMEM)
    return pl.pallas_call(
        guest_edges_body,
        out_shape=[z_out, z_out],
        in_specs=[vmem],
        out_specs=[vmem] * 2,
        scratch_shapes=[pltpu.VMEM((ny // 128, nx * nz, 128), jnp.float32)],
        compiler_params=pltpu.CompilerParams(vmem_limit_bytes=VMEM_LIMIT),
        name="guest_edges",
    )(hold(field))


def rows_to_matrix(sums, table, count, columns):
    lanes = lax.broadcasted_iota(jnp.int32, (count, 128), 1)
    zero = jnp.zeros((1, 128), jnp.float32)
    plain = jnp.zeros((count, 128), jnp.float32)
    moved = plain
    for i in range(count):
        if not any((i, j) in table for j in range(count)):
            continue
        stack = jnp.concatenate(
            [sums[table[i, j] : table[i, j] + 1] if (i, j) in table else zero for j in range(count)], axis=0
        )
        column = jnp.sum(stack, axis=1, keepdims=True)
        plain = jnp.where(lanes == i, column, plain)
        moved = jnp.where(lanes == (i + columns) % count, column, moved)
    return plain, moved


def pick_order(plain, moved, half_ref, columns):
    return jnp.where(half_ref[0] == 0, plain, pltpu.roll(moved, columns, 0))


def pair_sums(fields, pairs, acc, nx, three, ny):
    used = sorted({i for pair in pairs for i in pair})
    total = tuple(acc[p] for p in range(len(pairs)))
    for comp in range(three):

        def body(x, carry):
            for lane in range(0, ny, 128):
                cols = {i: fields[i][0][comp, fields[i][1], x, :, lane : lane + 128] for i in used}
                carry = tuple(c + cols[i] * cols[j] for c, (i, j) in zip(carry, pairs))
            return carry

        total = lax.fori_loop(0, nx, body, total, unroll=4)
    for p in range(len(pairs)):
        acc[p] = total[p]


def gram_tables(sums, acc, pairs):
    table = {}
    for p, (i, j) in enumerate(pairs):
        sums[p : p + 1] = jnp.sum(acc[p], axis=0, keepdims=True)
        table[i, j] = table[j, i] = p
    return table


def own_gram_body(half_ref, front_keep, front_send, late_keep, late_send, squares, out, acc, sums):
    three, front, nx, _, ny = front_keep.shape
    columns = front + late_keep.shape[1]
    count = 2 * columns
    pairs = [(i, j) for i in range(columns) for j in range(i, columns)]
    acc[...] = jnp.zeros_like(acc)
    for ahead, behind in ((front_keep, late_keep), (front_send, late_send)):
        fields = [(ahead, i) for i in range(front)] + [(behind, i) for i in range(columns - front)]
        pair_sums(fields, pairs, acc, nx, three, ny)
    plain, moved = rows_to_matrix(sums, gram_tables(sums, acc, pairs), count, columns)
    lanes = lax.broadcasted_iota(jnp.int32, (count, 128), 1)
    norm_rows = []
    for i in range(columns):
        rows = sum(squares[i, :, k : k + 128] for k in range(0, ny, 128))
        norm_rows.append(jnp.sum(rows, axis=0, keepdims=True))
    norm_rows += [jnp.zeros((1, 128), jnp.float32)] * columns
    norm = jnp.sum(jnp.concatenate(norm_rows, axis=0), axis=1, keepdims=True)
    plain = jnp.where(lanes == count, norm, plain)
    moved = jnp.where(lanes == count, norm, moved)
    out[...] = pick_order(plain, moved, half_ref, columns)


def cross_gram_body(half_ref, fk, fs, lk, ls, ek, es, other, base, out, acc, sums):
    three, front, nx, _, ny = fk.shape
    late = lk.shape[1]
    columns = front + late
    early = ek.shape[1]
    count = 2 * columns
    wide = [(i, columns + j) for i in range(columns) for j in range(early)]
    narrow = [(front + i, columns + early + j) for i in range(late) for j in range(columns - early)]
    acc[...] = jnp.zeros_like(acc)

    def own(ahead, behind):
        return [(ahead, i) for i in range(front)] + [(behind, i) for i in range(late)]

    for ahead, behind, extra in ((fk, lk, ek), (fs, ls, es)):
        pair_sums(own(ahead, behind) + [(extra, j) for j in range(early)], wide, acc, nx, three, ny)
    rest = acc.at[pl.ds(len(wide), len(narrow))]
    pair_sums(own(fk, lk) + [None] * early + [(other, j) for j in range(columns - early)], narrow, rest, nx, three, ny)
    for p, (i, j) in enumerate(wide):
        if i < early:
            acc[p] = jnp.where(half_ref[0] == 0, acc[p], 0.0)
    plain, moved = rows_to_matrix(sums, gram_tables(sums, acc, wide + narrow), count, columns)
    out[...] = base[...] + pick_order(plain, moved, half_ref, columns)


def run_gram(body, half, fields, npairs, count):
    nz = fields[0].shape[3]
    vmem = pl.BlockSpec(memory_space=pltpu.VMEM)
    return pl.pallas_call(
        body,
        out_shape=jax.ShapeDtypeStruct((count, 128), jnp.float32),
        in_specs=[pl.BlockSpec(memory_space=pltpu.SMEM)] + [vmem] * len(fields),
        out_specs=vmem,
        scratch_shapes=[pltpu.VMEM((npairs, nz, 128), jnp.float32), pltpu.VMEM((npairs, 128), jnp.float32)],
        compiler_params=pltpu.CompilerParams(vmem_limit_bytes=VMEM_LIMIT),
    )(half, *[hold(v) for v in fields])


def factor_body(entries, columns, half_ref, raw, factor, coef):
    side = step_length * viscosity
    count = 2 * columns
    total = raw[...]
    lanes = lax.broadcasted_iota(jnp.int32, (count, 128), 1)
    rows = lax.broadcasted_iota(jnp.int32, (count, 128), 0)
    scale = jnp.sqrt(total[:, count : count + 1] / entries + 1e-06)
    inverse_scale = side / scale
    scale_row = jnp.sum(jnp.where(lanes == rows, jnp.broadcast_to(scale, (count, 128)), 0.0), axis=0, keepdims=True)
    scale_row = jnp.where(lanes < count, jnp.broadcast_to(scale_row, (count, 128)), 1.0)
    gram = total * (side * side / entries) / (jnp.broadcast_to(scale, (count, 128)) * scale_row)
    work = jnp.where(lanes < count, gram, jnp.where(lanes == rows + count, 1.0, 0.0))
    for k in range(count):
        pivot = work[k : k + 1]
        root = jnp.sqrt(pivot[:, k : k + 1])
        line = pivot / root
        ratio = jnp.where(rows[:, 0:1] > k, work[:, k : k + 1], 0.0) / root
        work = jnp.where(rows == k, jnp.broadcast_to(line, (count, 128)), work - ratio * line)
    factor[...] = jnp.where(lanes >= rows, work, 0.0)[:, :count]
    first = half_ref[0] == 0
    for j in range(columns):
        row = jnp.where(first, work[j : j + 1], work[columns + j : columns + j + 1])
        for i in range(count):
            lo = (i + columns) % count
            pick = jnp.where(first, row[:, count + i : count + i + 1], row[:, count + lo : count + lo + 1])
            norm = jnp.where(first, inverse_scale[i : i + 1], inverse_scale[lo : lo + 1])
            coef[j * count + i] = jnp.broadcast_to(pick * norm, coef.shape[1:])


def run_factor(entries, columns, half, raw):
    count = 2 * columns
    vmem = pl.BlockSpec(memory_space=pltpu.VMEM)
    return pl.pallas_call(
        functools.partial(factor_body, entries, columns),
        out_shape=[
            jax.ShapeDtypeStruct((count, count), jnp.float32),
            jax.ShapeDtypeStruct((columns * count, 8, 128), jnp.float32),
        ],
        in_specs=[pl.BlockSpec(memory_space=pltpu.SMEM), vmem],
        out_specs=[vmem, vmem],
        compiler_params=pltpu.CompilerParams(vmem_limit_bytes=VMEM_LIMIT),
        name="factor",
    )(half, raw)


def basis_body(count, first, partial, aliased, half_ref, coef, *refs):
    fields, out = (refs[:-2], refs[-1]) if aliased else (refs[:-1], refs[-1])
    *fields, begun = fields if partial else (*fields, None)
    three, columns, nx, _, ny = out.shape
    base = 0 if out.shape[2] == fields[0].shape[2] else pl.program_id(0) * nx
    spots = [(ref, i) for ref in fields for i in range(ref.shape[1])]

    for comp in range(three):

        def body(x, _):
            for lane in range(0, ny, 128):
                part = slice(lane, lane + 128)
                cols = [ref[comp, i, base + x, :, part] for ref, i in spots]
                for j in range(columns):
                    terms = [coef[j * count + first + i] * c for i, c in enumerate(cols)]
                    if begun is not None:
                        terms.append(begun[comp, j, base + x, :, part])
                    while len(terms) > 1:
                        terms = [sum(terms[k : k + 2][1:], terms[k]) for k in range(0, len(terms), 2)]
                    out[comp, j, x, :, part] = terms[0]
            return 0

        lax.fori_loop(0, nx, body, 0, unroll=4)


def run_partial(half, coef, fields, columns, first):
    three, _, half_x, nz, ny = fields[0].shape
    vmem = pl.BlockSpec(memory_space=pltpu.VMEM)
    return pl.pallas_call(
        functools.partial(basis_body, 2 * columns, first, False, False),
        out_shape=in_vmem((three, columns, half_x, nz, ny)),
        in_specs=[pl.BlockSpec(memory_space=pltpu.SMEM)] + [vmem] * (len(fields) + 1),
        out_specs=vmem,
        compiler_params=pltpu.CompilerParams(vmem_limit_bytes=VMEM_LIMIT),
        name="partial",
    )(half, *[hold(v) for v in (coef, *fields)])


def run_basis(half, coef, fields, columns, keep, target=None, begun=None, first=0):
    three, _, half_x, nz, ny = fields[0].shape
    per = 2
    block = (three, columns, half_x // per, nz, ny)
    vmem = pl.BlockSpec(memory_space=pltpu.VMEM)

    def place(k, h):
        return (0, 0, k + per * (h[0] if keep else 1 - h[0]), 0, 0)

    if begun is not None:
        fields = (*fields, begun)
    operands = [hold(v) for v in (coef, *fields)]
    specs = [vmem] * len(operands)
    if target is not None:
        operands, specs = operands + [target], specs + [pl.BlockSpec(memory_space=pl.ANY)]
    return pl.pallas_call(
        functools.partial(basis_body, 2 * columns, first, begun is not None, target is not None),
        out_shape=jax.ShapeDtypeStruct((three, columns, 2 * half_x, nz, ny), jnp.float32),
        grid_spec=pltpu.PrefetchScalarGridSpec(
            num_scalar_prefetch=1, grid=(per,), in_specs=specs, out_specs=pl.BlockSpec(block, place)
        ),
        input_output_aliases={} if target is None else {len(operands): 0},
        compiler_params=pltpu.CompilerParams(vmem_limit_bytes=VMEM_LIMIT),
        name="basis",
    )(half, *operands)


def shift(value, axis, amount):
    count = lax.axis_size(axis)
    return lax.ppermute(value, axis, [(i, (i + amount) % count) for i in range(count)])


def exchange(first_z, last_z, first_x=None, last_x=None):
    zlo = shift(last_z, "gz", 1)
    zhi = shift(first_z, "gz", -1)
    if first_x is None:
        return zlo, zhi
    xlo = shift(last_x, "gx", 1)
    xhi = shift(first_x, "gx", -1)
    return zlo, zhi, xlo, xhi


def partner(value, axis, count, mask):
    return lax.ppermute(value, axis, [(i, i ^ mask) for i in range(count)])


def all_sum(value, axes, wide):
    for axis in axes:
        count = lax.axis_size(axis)
        if count & (count - 1):
            value = lax.psum(value, axis)
            continue
        mask = 1
        while mask < count:
            if wide == axis and 4 * mask <= count:
                near, far, both = (partner(value, axis, count, k * mask) for k in (1, 2, 3))
                value = (value + near) + (far + both)
                mask *= 4
            else:
                value = value + partner(value, axis, count, mask)
                mask *= 2
    return value


def swap(value):
    return lax.ppermute(value, "sa", [(0, 1), (1, 0)])


def shards(forcing, velocity, wall_solve):
    columns, nx, nz, ny = forcing.shape[1:]
    entries = float(3 * nx * lax.axis_size("gx") * nz * lax.axis_size("gz") * ny)
    half = lax.axis_index("sa").astype(jnp.int32).reshape(1)
    early = columns // 2
    count = 2 * columns
    forcing, front, *edge = run_edges(forcing, half, early)
    guest = swap(front)
    faces = exchange(*edge)
    coef, wall = run_setup(wall_solve, velocity, nz)

    def stage(kind, *args, **kwargs):
        return run_stage(kind, half, *args, **kwargs)

    relay, q1, *edge = stage("forward_first", forcing, None, faces, coef, wall, relay=early)
    faces = exchange(*edge)
    side1 = swap(relay)
    relay, q2, s1, *edge, squares = stage("forward_last", q1, forcing, faces, coef, wall, squares=True, relay=early)
    faces = exchange(*edge)
    side2 = swap(relay)
    relay, s2, *edge = stage("adjoint_first", s1, q2, faces, coef, wall, relay=early)
    faces = exchange(*edge)
    side3 = swap(run_relay(relay, *faces[2:]))
    late_keep, late_send = stage("adjoint_last", s2, q2, faces, coef, wall, span=(early, columns))
    other_keep = swap(late_send)
    front_keep, front_send = stage("adjoint_last", s2, q2, faces, coef, wall, span=(0, early))

    edge = run_guest_edges(guest)
    faces = exchange(*edge)
    g1, *edge = stage("forward_first", guest, None, (*faces, side1), coef, wall)
    faces = exchange(*edge)
    g2, h1, *edge = stage("forward_last", g1, guest, (*faces, side2), coef, wall)
    faces = exchange(*edge)
    h2, *edge = stage("adjoint_first", h1, g2, (*faces, side3), coef, wall)
    faces = exchange(*edge)
    early_keep, early_send = stage("adjoint_last", h2, g2, (*faces, side3), coef, wall, place=1)

    own = (front_keep, front_send, late_keep, late_send)
    base = run_gram(own_gram_body, half, (*own, squares), columns * (columns + 1) // 2, count)
    late_keep, other_keep = lax.optimization_barrier((late_keep, other_keep))
    other_send = swap(late_keep)
    cross = (*own, early_keep, early_send, other_keep, base)
    npairs = columns * early + (columns - early) ** 2
    raw = run_gram(cross_gram_body, half, cross, npairs, count)
    raw = all_sum(raw, ("sa",), "gz")
    raw = all_sum(raw, ("gx",), "gz")
    raw = all_sum(raw, ("gz",), "gz")
    factor, coef = run_factor(entries, columns, half, raw)
    basis = run_basis(half, coef, (front_keep, late_keep, early_keep, other_keep), columns, True)
    begun = run_partial(half, coef, (front_send, late_send, early_send), columns, 0)
    basis = run_basis(half, coef, (other_send,), columns, False, basis, begun, columns + early)
    return basis, factor


def solution(mesh):
    return jax.shard_map(
        shards,
        mesh=mesh,
        in_specs=(P(None, "sa", "gx", "gz", None), P(), P()),
        out_specs=(P(None, "sa", "gx", "gz", None), P()),
        check_vma=False,
    )
```
